32 devices in a mesh: rows: 4 (over y, core), cols: 8 (over z, x).
Axes of the slice: x: 2, y: 2, z: 4, core: 2. Of those that a mesh axis runs over, the one named last changes fastest.
Arguments:
- prior: float32 [64, 512, 512], P('rows', 'cols'), may hold values from -6 to 6
- obs_cell: int32 [8, 128], replicated, may hold values from 0 to 32767, as said below
- obs_weight: float32 [8, 128, 8], replicated, may hold values from 0.1 to 1
- obs_value: float32 [8, 128], replicated, may hold values from -8 to 8
- obs_var: float32 [8, 128], replicated, may hold values from 0.25 to 4
- loc_mask: int32 [8, 32], replicated, may hold values from 0 to 1, as said below
- batch_order: int32 [8], replicated, may hold values from 0 to 7, each once
- kernel: float32 [8, 7, 7], replicated, may hold values from 0.005 to 0.04
- mixing: float32 [8, 8], replicated, may hold values from -2 to 2
Outputs:
- forecast: float32 [64, 512, 512], P('rows', 'cols')
The draws below stay inside these ranges and needn't reach their ends.
Inputs may be any that keep to these rules, and one draw needn't show every extreme that they name: `obs_cell`: all 128 cells of one batch lie in one tile, rows r * 16 to (r + 1) * 16 - 1 and columns c * 64 to (c + 1) * 64 - 1, whose index is r * 8 + c. `loc_mask`: for each batch the tiles marked 1 form a rectangle of tiles that contains the tile of that batch's cells. `batch_order`: each batch appears once.
All inputs are finite; a program needn't handle non-finite values.
Results may differ from the reference program's by a relative error of at most 0.0003.
Values sent between devices are 32-bit elements; how exact they have to be, the bound alone decides.
No kernel may reach another device: no remote copies, remote signals or barrier semaphores. Data moves between devices by JAX's collectives and lax.ppermute only.
A program may use at most 128 MiB of HBM per device.

```python
import math
import jax
import jax.numpy as jnp
from jax import lax

SPECIES = 8
MEMBERS = 64
ROWS_DEV = 16
COLS_DEV = 64
OBS = 128
BATCHES = 8
KW = 7
HALFW = 48
NY = 64
NX = 512
N_ROWS = 4
N_COLS = 8


def placement_plan(key):
    base = jax.random.fold_in(key, 4111)
    keys = jax.random.split(base, 7)
    tile_rows = NY // ROWS_DEV
    tile_cols = NX // COLS_DEV
    centre_row = jax.random.randint(keys[0], (), 1, tile_rows - 1)
    centre_col = jax.random.randint(keys[1], (), 1, tile_cols - 1)
    owner_row = centre_row + jax.random.randint(keys[2], (BATCHES,), -1, 2)
    owner_col = centre_col + jax.random.randint(keys[3], (BATCHES,), -1, 2)
    reach_row = jax.random.randint(keys[4], (BATCHES,), 1, 4)
    reach_col = jax.random.randint(keys[5], (BATCHES,), 1, 3)
    return (owner_row, owner_col, reach_row, reach_col, keys[6])


def draw_obs_cell(key, part):
    owner_row, owner_col, reach_row, reach_col, cell_key = placement_plan(key)
    first_key, second_key = jax.random.split(cell_key)
    cell_rows = owner_row[:, None] * ROWS_DEV + jax.random.randint(first_key, (BATCHES, OBS), 0, ROWS_DEV)
    cell_cols = owner_col[:, None] * COLS_DEV + jax.random.randint(second_key, (BATCHES, OBS), 0, COLS_DEV)
    return (cell_rows * NX + cell_cols).astype(jnp.int32)


def draw_loc_mask(key, part):
    owner_row, owner_col, reach_row, reach_col, cell_key = placement_plan(key)
    tile_rows = NY // ROWS_DEV
    tile_cols = NX // COLS_DEV
    row_ids = jnp.arange(tile_rows, dtype=jnp.int32)[None, :, None]
    col_ids = jnp.arange(tile_cols, dtype=jnp.int32)[None, None, :]
    inside_rows = jnp.abs(row_ids - owner_row[:, None, None]) <= reach_row[:, None, None]
    inside_cols = jnp.abs(col_ids - owner_col[:, None, None]) <= reach_col[:, None, None]
    marked = jnp.logical_and(inside_rows, inside_cols)
    return marked.reshape(BATCHES, tile_rows * tile_cols).astype(jnp.int32)


def steps_of(rng, dims, pieces, low, largest):
    def one(dim, blocks):
        steps = jax.random.uniform(jax.random.fold_in(jax.random.fold_in(rng, 6), dim), (blocks,), jnp.float32, low / len(pieces), largest / len(pieces))
        return jnp.repeat(jnp.exp(steps), dims[dim] // blocks).reshape((-1,) + (1,) * (len(dims) - dim - 1))

    level = one(*pieces[0])
    for cut in pieces[1:]:
        level = level * one(*cut)
    return level


def scatter_about(key, extent, deviation, limit, cuts=(), held_as=jnp.bfloat16):
    factor_of = steps_of(key, extent, cuts, -0.22, 0.18) if cuts else 1.0
    array = jax.random.normal(key, extent, jnp.float32) * deviation * factor_of
    return jnp.minimum(jnp.maximum(array, -limit), limit).astype(held_as)


def setup_inputs(seed: int = 0) -> dict:
    seeds = jax.random.split(jax.random.key(seed), 10)
    return {
        "prior": scatter_about(seeds[0], (NY, NX, SPECIES * MEMBERS), 1.0, 6.0, ((0, 4), (1, 8)), jnp.float32),
        "obs_cell": draw_obs_cell(jax.random.fold_in(seeds[9], 71), 0),
        "obs_weight": jnp.clip(jnp.exp(jax.random.uniform(seeds[2], (BATCHES, OBS, SPECIES), jnp.float32, math.log(0.1), math.log(1.0))), 0.1, 1.0),
        "obs_value": scatter_about(seeds[3], (BATCHES, OBS), 2.0, 8.0, (), jnp.float32),
        "obs_var": jnp.clip(jnp.exp(jax.random.uniform(seeds[4], (BATCHES, OBS), jnp.float32, math.log(0.25), math.log(4.0))), 0.25, 4.0),
        "loc_mask": draw_loc_mask(jax.random.fold_in(seeds[9], 71), 0),
        "batch_order": jax.random.permutation(seeds[6], BATCHES).astype(jnp.int32),
        "kernel": jnp.clip(jax.random.uniform(seeds[7], (SPECIES, KW, KW), jnp.float32, 0.005, 0.04), 0.005, 0.04),
        "mixing": scatter_about(seeds[8], (SPECIES, SPECIES), SPECIES ** -0.5, 2.0, (), jnp.float32),
    }


def taper_weights(ratio):
    clamped = jnp.maximum(ratio, 1.0)
    inner_part = (((-0.25 * ratio + 0.5) * ratio + 0.625) * ratio - 5.0 / 3.0) * ratio * ratio + 1.0
    outer_part = ((((ratio / 12.0 - 0.5) * ratio + 0.625) * ratio + 5.0 / 3.0) * ratio - 5.0) * ratio + 4.0 - 2.0 / (3.0 * clamped)
    return jnp.where(ratio <= 1.0, inner_part, jnp.where(ratio < 2.0, outer_part, 0.0))

def batch_gain(predicted, value_row, var_row):
    mean_pred = lax.optimization_barrier(jnp.mean(predicted, axis=1))
    spread = predicted - mean_pred[:, None]
    variance = lax.optimization_barrier(jnp.sum(spread * spread, axis=1)) / (predicted.shape[1] - 1)
    denominator = variance + var_row
    shrink = 1.0 / (1.0 + jnp.sqrt(var_row / denominator))
    kalman_gain = ((value_row - mean_pred)[:, None] - shrink[:, None] * spread) / denominator[:, None]
    return (spread, kalman_gain)

def refresh_block(block, first_row, first_col, cell_row, cell_col, spread, kalman_gain, active):
    rows_count, cols_count, channels = block.shape
    members = spread.shape[1]
    species = channels // members
    row_pos = (first_row + jnp.arange(rows_count, dtype=jnp.int32)).astype(jnp.float32)
    col_pos = (first_col + jnp.arange(cols_count, dtype=jnp.int32)).astype(jnp.float32)
    row_gap = row_pos[:, None, None] - cell_row.astype(jnp.float32)[None, None, :]
    col_gap = col_pos[None, :, None] - cell_col.astype(jnp.float32)[None, None, :]
    squared = row_gap * row_gap + col_gap * col_gap
    taper = taper_weights(jnp.sqrt(squared) / HALFW) * active
    taper = taper.reshape(rows_count * cols_count, cell_row.shape[0])
    members_view = block.reshape(rows_count * cols_count, species, members)
    covariance = jnp.einsum('psm,im->psi', members_view, spread, precision=lax.Precision.HIGHEST) / (members - 1)
    increment = jnp.einsum('psi,im->psm', covariance * taper[:, None, :], kalman_gain, precision=lax.Precision.HIGHEST)
    return (members_view + increment).reshape(rows_count, cols_count, channels)

def reference(prior, obs_cell, obs_weight, obs_value, obs_var, loc_mask, batch_order, kernel, mixing):
    species = kernel.shape[0]
    channels = prior.shape[2]
    members = channels // species
    ensemble = prior
    for position in range(BATCHES):
        current = batch_order[position]
        obs_cells = obs_cell[current]
        flat_view = ensemble.reshape(NY * NX, species, members)
        picked = flat_view[obs_cells]
        predicted = jnp.einsum('is,ism->im', obs_weight[current], picked, precision=lax.Precision.HIGHEST)
        spread, kalman_gain = batch_gain(predicted, obs_value[current], obs_var[current])
        cell_row = (obs_cells // NX).astype(jnp.int32)
        cell_col = (obs_cells % NX).astype(jnp.int32)
        mask_row = loc_mask[current]

        def visit(tile, field, cell_row=cell_row, cell_col=cell_col, spread=spread, kalman_gain=kalman_gain, mask_row=mask_row):
            tile_row = tile // N_COLS
            tile_col = tile % N_COLS
            first_row = (tile_row * ROWS_DEV).astype(jnp.int32)
            first_col = (tile_col * COLS_DEV).astype(jnp.int32)
            zero_index = jnp.zeros((), jnp.int32)

            def update(field_in):
                block = lax.dynamic_slice(field_in, (first_row, first_col, zero_index), (ROWS_DEV, COLS_DEV, channels))
                fresh = refresh_block(block, first_row, first_col, cell_row, cell_col, spread, kalman_gain, jnp.float32(1.0))
                return lax.dynamic_update_slice(field_in, fresh, (first_row, first_col, zero_index))

            def keep_field(field_in):
                return field_in
            return lax.cond(mask_row[tile] > 0, update, keep_field, field)
        ensemble = lax.fori_loop(0, N_ROWS * N_COLS, visit, ensemble)
    halo_width = KW // 2
    grid_view = ensemble.reshape(NY, NX, species, members)
    padded = jnp.pad(grid_view, ((halo_width, halo_width), (halo_width, halo_width), (0, 0), (0, 0)))
    smoothed = jnp.zeros_like(grid_view)
    for vertical in range(KW):
        for lateral in range(KW):
            smoothed = smoothed + kernel[:, vertical, lateral][None, None, :, None] * padded[vertical:vertical + NY, lateral:lateral + NX]
    mixed_field = jnp.einsum('st,yxtm->yxsm', mixing, smoothed, precision=lax.Precision.HIGHEST)
    return mixed_field.reshape(NY, NX, channels)
```

```python
import functools

import jax
import jax.numpy as jnp
from jax import lax
from jax.experimental import pallas as pl
from jax.experimental.pallas import tpu as pltpu
from jax.sharding import PartitionSpec as P

BATCHES = 8
OBS = 128
SPECIES = 8
MEMBERS = 64
KW = 7
HALO = KW // 2
HALFW = 48
BF16 = jnp.bfloat16
F32 = jnp.float32
VMEM = pl.BlockSpec(memory_space=pltpu.VMEM)
SMEM = pl.BlockSpec(memory_space=pltpu.SMEM)
PARAMS = pltpu.CompilerParams(vmem_limit_bytes=56 << 20)


def split(x):
    high = x.astype(BF16)
    return high, (x - high.astype(F32)).astype(BF16)


def dot(a, b):
    return jnp.dot(a, b, preferred_element_type=F32)


def swap_halves(x):
    return pltpu.roll(x, MEMBERS, axis=x.ndim - 1)


def low_lanes(shape):
    return lax.broadcasted_iota(jnp.int32, shape, len(shape) - 1) < MEMBERS


def taper_weights(squared):
    inverse = lax.rsqrt(jnp.maximum(squared, 1.0))
    ratio = squared * inverse * (1.0 / HALFW)
    outer_inverse = (2.0 * HALFW / 3.0) * inverse
    inner = (((-0.25 * ratio + 0.5) * ratio + 0.625) * ratio - 5.0 / 3.0) * ratio * ratio + 1.0
    outer = (
        ((((ratio * (1.0 / 12.0) - 0.5) * ratio + 0.625) * ratio + 5.0 / 3.0) * ratio - 5.0) * ratio
        + 4.0
        - outer_inverse
    )
    return jnp.where(ratio <= 1.0, inner, jnp.where(ratio < 2.0, outer, 0.0))


def place(cols_count):
    return lax.axis_index("rows"), lax.axis_index("cols")


def gather_kernel(width, order, cells, weight_ref, prior_ref, out_ref, picked):
    height, cols = prior_ref.shape[0], prior_ref.shape[1]
    my_row, my_col = lax.axis_index("rows"), lax.axis_index("cols")
    mine = 2 * lax.rem(my_row, 2) + lax.rem(lax.div(my_row, 2), 2)
    out_ref[...] = jnp.zeros_like(out_ref)
    for k in range(BATCHES):
        batch = order[k]
        first = cells[batch, 0]
        owner = (lax.div(first, width * height) == my_row) & (
            lax.div(lax.rem(first, width), cols) == my_col
        )

        @pl.when(owner)
        def _():
            def one(i, carry):
                cell = cells[batch, i]
                row = lax.div(cell, width) - my_row * height
                col = lax.rem(cell, width) - my_col * cols
                picked[pl.ds(i, 1), :] = prior_ref[row, pl.ds(col, 1), :]
                return carry

            lax.fori_loop(0, OBS, one, 0, unroll=8)
            weights = weight_ref[batch]
            low = low_lanes((OBS, 2 * MEMBERS))
            total = jnp.zeros((OBS, 2 * MEMBERS), F32)
            for p in range(SPECIES // 2):
                scale = jnp.where(low, weights[:, 2 * p : 2 * p + 1], weights[:, 2 * p + 1 : 2 * p + 2])
                total = total + scale * picked[:, 128 * p : 128 * (p + 1)]
            total = total + swap_halves(total)
            slot = jnp.bitwise_xor(k % 4, mine)
            keep = low if k < 4 else jnp.logical_not(low)
            out_ref[slot] = jnp.where(keep, total, out_ref[slot])


def exchange(parts):
    size = lax.axis_size("rows")
    cols = lax.axis_size("cols")

    def rows(x, bit):
        return lax.ppermute(x, "rows", [(i, i ^ bit) for i in range(size)])

    kept = parts[:2] + rows(parts[2:], 1)
    kept = kept[0] + rows(kept[1], 2)
    bit = 4
    while bit < size:
        kept = kept + rows(kept, bit)
        bit *= 2
    bit = 1
    while bit < cols:
        kept = kept + lax.ppermute(kept, "cols", [(i, i ^ bit) for i in range(cols)])
        bit *= 2
    other = rows(kept, 2)
    return kept, other, rows(kept, 1), rows(other, 1)


def main_kernel(
    width, order, cells, mask, cell_ref, value_ref, var_ref, prior_ref, p0, p1, p2, p3,
    out_ref, left_ref, right_ref, predicted, table,
):
    height, cols = prior_ref.shape[0], prior_ref.shape[1]
    my_row, my_col = lax.axis_index("rows"), lax.axis_index("cols")
    across = width // cols
    my_tile = my_row * across + my_col
    mine = 2 * lax.rem(my_row, 2) + lax.rem(lax.div(my_row, 2), 2)
    for rel, part in enumerate((p0, p1, p2, p3)):
        predicted[jnp.bitwise_xor(rel, mine)] = part[...]
    low = low_lanes((cols, 2 * MEMBERS))
    for j in range(height // 2):
        for p in range(SPECIES // 2):
            a = prior_ref[2 * j, :, 128 * p : 128 * (p + 1)]
            b = prior_ref[2 * j + 1, :, 128 * p : 128 * (p + 1)]
            out_ref[j, 2 * p * cols : (2 * p + 1) * cols] = jnp.where(low, a, swap_halves(b))
            out_ref[j, (2 * p + 1) * cols : (2 * p + 2) * cols] = jnp.where(low, swap_halves(a), b)
    batches = [order[k] for k in range(BATCHES)]
    tiles = []
    for k in range(BATCHES):
        first = cells[batches[k], 0]
        tiles.append(lax.div(first, width * height) * across + lax.div(lax.rem(first, width), cols))
        table[k : k + 1, :] = cell_ref[pl.ds(batches[k], 1), :].astype(F32)
        table[8 + k : 9 + k, :] = value_ref[pl.ds(batches[k], 1), :]
        table[16 + k : 17 + k, :] = var_ref[pl.ds(batches[k], 1), :]
    cell_lane = table[0:8, :]
    row_lane = jnp.floor(cell_lane * (1.0 / width))
    col_lane = cell_lane - row_lane * width
    row_col = jnp.transpose(row_lane)
    col_col = jnp.transpose(col_lane)
    value_col = jnp.transpose(table[8:16, :])
    var_col = jnp.transpose(table[16:24, :])
    low_obs = low_lanes((OBS, 2 * MEMBERS))
    x_pos = (my_col * cols + lax.broadcasted_iota(jnp.int32, (cols, OBS), 0)).astype(F32)

    def update(x, taper, spread_w, spread_lo, gain_w, gain_hi):
        high, low_part = split(x)
        cov = dot(jnp.concatenate([high, low_part], 1), spread_w) + dot(high, spread_lo)
        c_high, c_low = split(cov * taper)
        both = dot(c_high, gain_w)
        return x + (both[:, : 2 * MEMBERS] + both[:, 2 * MEMBERS :] + dot(c_low, gain_hi))

    for k in range(BATCHES):
        block = predicted[k % 4]
        if k < 4:
            here = jnp.where(low_obs, block, swap_halves(block))
        else:
            here = jnp.where(low_obs, swap_halves(block), block)
        mean = jnp.sum(here, axis=1, keepdims=True) * (0.5 / MEMBERS)
        spread = here - mean
        variance = jnp.sum(spread * spread, axis=1, keepdims=True) * (0.5 / (MEMBERS - 1))
        var = var_col[:, k : k + 1]
        denominator = variance + var
        shrink = 1.0 / (1.0 + jnp.sqrt(var / denominator))
        gain = ((value_col[:, k : k + 1] - mean) - shrink * spread) / (
            denominator * (MEMBERS - 1)
        )
        turned = jnp.transpose(spread)
        top = lax.broadcasted_iota(jnp.int32, turned.shape, 0) < MEMBERS
        zero = jnp.zeros_like(turned)
        wide = jnp.concatenate([jnp.where(top, turned, zero), jnp.where(top, zero, turned)], 1)
        wide_hi, wide_lo = split(wide)
        spread_w = jnp.concatenate([wide_hi, wide_hi], 0)
        tall = jnp.concatenate([jnp.where(low_obs, gain, zero), jnp.where(low_obs, zero, gain)], 0)
        tall_hi, tall_lo = split(tall)
        gain_w = jnp.concatenate([tall_hi, tall_lo], 1)
        obs_row, obs_col = row_lane[k : k + 1, :], col_lane[k : k + 1, :]
        if k < BATCHES - 1:
            for q in range(4):
                if q + 4 <= k:
                    continue
                halves = []
                for later in (q, q + 4):
                    dr = row_col[:, later : later + 1] - obs_row
                    dc = col_col[:, later : later + 1] - obs_col
                    active = (mask[batches[k], tiles[later]] > 0).astype(F32)
                    halves.append(taper_weights(dr * dr + dc * dc) * active)
                predicted[q] = update(
                    predicted[q], jnp.concatenate(halves, 1), spread_w, wide_lo, gain_w, tall_hi
                )

        @pl.when(mask[batches[k], my_tile] > 0)
        def _():
            dx = x_pos - obs_col
            dx = dx * dx

            def pair(j, carry):
                halves = []
                for h in range(2):
                    dy = (my_row * height + 2 * j + h).astype(F32) - obs_row
                    halves.append(taper_weights(dx + dy * dy))
                taper = jnp.concatenate(halves, 1)
                taper = jnp.concatenate([taper] * SPECIES, 0)
                out_ref[j] = update(out_ref[j], taper, spread_w, wide_lo, gain_w, tall_hi)
                return carry

            lax.fori_loop(0, height // 2, pair, 0)

    for j in range(height // 2):
        for e in range(HALO):
            for t in range(SPECIES):
                left_ref[j, e, t : t + 1, :] = out_ref[j, t * cols + e : t * cols + e + 1, :]
                r = t * cols + cols - HALO + e
                right_ref[j, e, t : t + 1, :] = out_ref[j, r : r + 1, :]


def smooth_kernel(kern, mix, tile_ref, left_ref, right_ref, up_ref, down_ref, out_ref, padded, lines):
    pairs, cols = tile_ref.shape[0], tile_ref.shape[1] // SPECIES
    depth = cols + 16
    lanes = 2 * MEMBERS
    half = 3 * SPECIES
    edge = jnp.zeros((8, lanes), F32)
    for q in range(pairs + 4):
        for t in range(SPECIES):
            padded[q, t, 0:8, :] = edge
            padded[q, t, depth - 8 : depth, :] = edge
            if q < 2:
                body = up_ref[q, t * cols : (t + 1) * cols, :]
            elif q < pairs + 2:
                body = tile_ref[q - 2, t * cols : (t + 1) * cols, :]
            else:
                body = down_ref[q - pairs - 2, t * cols : (t + 1) * cols, :]
            padded[q, t, 8 : 8 + cols, :] = body
            for e in range(HALO):
                at = e * SPECIES + t
                base = SPECIES * cols
                if q < 2:
                    a = up_ref[q, base + at : base + at + 1, :]
                    b = up_ref[q, base + half + at : base + half + at + 1, :]
                elif q < pairs + 2:
                    a = left_ref[q - 2, e, t : t + 1, :]
                    b = right_ref[q - 2, e, t : t + 1, :]
                else:
                    a = down_ref[q - pairs - 2, base + at : base + at + 1, :]
                    b = down_ref[q - pairs - 2, base + half + at : base + half + at + 1, :]
                padded[q, t, 5 + e : 6 + e, :] = a
                padded[q, t, 8 + cols + e : 9 + cols + e, :] = b
    offset = lax.broadcasted_iota(jnp.int32, (cols, depth), 1) - (
        lax.broadcasted_iota(jnp.int32, (cols, depth), 0) + 5
    )
    low = low_lanes((cols, lanes))

    def species(t, carry):
        bands = []
        for a in range(KW):
            band = jnp.zeros((cols, depth), F32)
            for e in range(KW):
                band = jnp.where(offset == e, kern[t, a * KW + e], band)
            bands.append(band)
        band_hi, band_lo = split(jnp.concatenate(bands, 0))
        for d in range(0, pairs + 4, 2):
            data = jnp.concatenate([padded[d, t], padded[d + 1, t]], 1)
            hi, lo = split(data)
            product = dot(band_hi, hi) + dot(band_hi, lo) + dot(band_lo, hi)
            lines[d] = product[:, :lanes]
            lines[d + 1] = product[:, lanes:]

        def part(q, a):
            return lines[q, a * cols : (a + 1) * cols, :]

        def odd(u):
            return swap_halves(part(u, 0) + part(u + 1, 2) + part(u + 2, 4) + part(u + 3, 6))

        before = odd(0)
        for j in range(pairs):
            after = odd(j + 1)
            straight = part(j + 1, 1) + part(j + 2, 3) + part(j + 3, 5)
            padded[j, t, 0:cols, :] = straight + jnp.where(low, before, after)
            before = after
        return carry

    lax.fori_loop(0, SPECIES, species, 0)

    def mixed(j, carry):
        smooth = [padded[j, t, 0:cols, :] for t in range(SPECIES)]
        for p in range(SPECIES // 2):
            total = []
            for s in (2 * p, 2 * p + 1):
                acc = mix[s, 0] * smooth[0]
                for t in range(1, SPECIES):
                    acc = acc + mix[s, t] * smooth[t]
                total.append(acc)
            out_ref[2 * j, :, 128 * p : 128 * (p + 1)] = jnp.where(low, total[0], swap_halves(total[1]))
            out_ref[2 * j + 1, :, 128 * p : 128 * (p + 1)] = jnp.where(
                low, swap_halves(total[0]), total[1]
            )
        return carry

    lax.fori_loop(0, pairs, mixed, 0)


def shards(prior, obs_cell, obs_weight, obs_value, obs_var, loc_mask, batch_order, kernel, mixing):
    height, cols, channels = prior.shape
    across = lax.axis_size("cols")
    width = cols * across
    pairs = height // 2
    lanes = 2 * MEMBERS
    parts = pl.pallas_call(
        functools.partial(gather_kernel, width),
        out_shape=jax.ShapeDtypeStruct((4, OBS, lanes), F32),
        in_specs=[SMEM, SMEM, VMEM, VMEM],
        out_specs=VMEM,
        scratch_shapes=[pltpu.VMEM((OBS, channels), F32)],
        compiler_params=PARAMS,
        name="gather",
    )(batch_order, obs_cell, obs_weight, prior)
    arrived = exchange(parts)
    tile, left, right = pl.pallas_call(
        functools.partial(main_kernel, width),
        out_shape=(
            jax.ShapeDtypeStruct((pairs, SPECIES * cols, lanes), F32),
            jax.ShapeDtypeStruct((pairs, HALO, SPECIES, lanes), F32),
            jax.ShapeDtypeStruct((pairs, HALO, SPECIES, lanes), F32),
        ),
        in_specs=[SMEM] * 3 + [VMEM] * 8,
        out_specs=(VMEM, VMEM, VMEM),
        scratch_shapes=[pltpu.VMEM((4, OBS, lanes), F32), pltpu.VMEM((24, OBS), F32)],
        compiler_params=PARAMS,
        name="assimilate",
    )(batch_order, obs_cell, loc_mask, obs_cell, obs_value, obs_var, prior, *arrived)

    def shift(x, axis, step):
        size = lax.axis_size(axis)
        return lax.ppermute(
            x, axis, [(i, i + step) for i in range(size) if 0 <= i + step < size]
        )

    from_left = shift(right, "cols", 1)
    from_right = shift(left, "cols", -1)

    def with_sides(lo, hi):
        flat = (hi - lo, HALO * SPECIES, lanes)
        return jnp.concatenate(
            [tile[lo:hi], from_left[lo:hi].reshape(flat), from_right[lo:hi].reshape(flat)], 1
        )

    above = shift(with_sides(pairs - 2, pairs), "rows", 1)
    below = shift(with_sides(0, 2), "rows", -1)
    return pl.pallas_call(
        smooth_kernel,
        out_shape=jax.ShapeDtypeStruct((height, cols, channels), F32),
        in_specs=[SMEM, SMEM] + [VMEM] * 5,
        out_specs=VMEM,
        scratch_shapes=[
            pltpu.VMEM((pairs + 4, SPECIES, cols + 16, lanes), F32),
            pltpu.VMEM((pairs + 4, KW * cols, lanes), F32),
        ],
        compiler_params=PARAMS,
        name="smooth",
    )(kernel.reshape(SPECIES, KW * KW), mixing, tile, from_left, from_right, above, below)


def solution(mesh):
    return jax.shard_map(
        shards,
        mesh=mesh,
        in_specs=(P("rows", "cols", None), P(), P(), P(), P(), P(), P(), P(), P()),
        out_specs=P("rows", "cols", None),
        check_vma=False,
    )
```

```python
import functools

import jax
import jax.numpy as jnp
from jax import lax
from jax.experimental import pallas as pl
from jax.experimental.pallas import tpu as pltpu
from jax.sharding import PartitionSpec as P

BATCHES = 8
OBS = 128
SPECIES = 8
MEMBERS = 64
KW = 7
HALO = KW // 2
HALFW = 48
BF16 = jnp.bfloat16
F32 = jnp.float32
VMEM = pl.BlockSpec(memory_space=pltpu.VMEM)
SMEM = pl.BlockSpec(memory_space=pltpu.SMEM)
PARAMS = pltpu.CompilerParams(vmem_limit_bytes=56 << 20)


def split(x):
    high = x.astype(BF16)
    return high, (x - high.astype(F32)).astype(BF16)


def dot(a, b):
    return jnp.dot(a, b, preferred_element_type=F32)


def swap_halves(x):
    return pltpu.roll(x, MEMBERS, axis=x.ndim - 1)


def low_lanes(shape):
    return lax.broadcasted_iota(jnp.int32, shape, len(shape) - 1) < MEMBERS


def taper_weights(squared):
    inverse = lax.rsqrt(jnp.maximum(squared, 1e-4))
    ratio = squared * inverse
    inner = 1.0 - (ratio * ratio) * (5.0 / 3.0 - ratio * (0.625 + ratio * (0.5 - 0.25 * ratio)))
    left = jnp.maximum(2.0 - ratio, 0.0)
    left = left * left
    outer = (left * left) * (((ratio + 2.0) * ratio - 0.5) * (inverse * (1.0 / 12.0)))
    return jnp.where(ratio <= 1.0, inner, outer)


def gather_kernel(width, order, cells, weight_ref, prior_ref, kept_ref, sent_ref, picked):
    height, cols = prior_ref.shape[0], prior_ref.shape[1]
    my_row, my_col = lax.axis_index("rows"), lax.axis_index("cols")
    mine = 2 * lax.rem(my_row, 2) + lax.rem(lax.div(my_row, 2), 2)
    kept_ref[...] = jnp.zeros_like(kept_ref)
    sent_ref[...] = jnp.zeros_like(sent_ref)
    for k in range(BATCHES):
        batch = order[k]
        first = cells[batch, 0]
        owner = (lax.div(first, width * height) == my_row) & (
            lax.div(lax.rem(first, width), cols) == my_col
        )

        @pl.when(owner)
        def _():
            def one(i, carry):
                cell = cells[batch, i]
                row = lax.div(cell, width) - my_row * height
                col = lax.rem(cell, width) - my_col * cols
                picked[pl.ds(i, 1), :] = prior_ref[row, pl.ds(col, 1), :]
                return carry

            lax.fori_loop(0, OBS, one, 0, unroll=8)
            weights = jnp.transpose(weight_ref[batch])
            low = low_lanes((OBS, 2 * MEMBERS))
            total = jnp.zeros((OBS, 2 * MEMBERS), F32)
            for p in range(SPECIES // 2):
                scale = jnp.where(low, weights[:, 2 * p : 2 * p + 1], weights[:, 2 * p + 1 : 2 * p + 2])
                total = total + scale * picked[:, 128 * p : 128 * (p + 1)]
            total = total + swap_halves(total)
            slot = jnp.bitwise_xor(k % 4, mine)
            keep = low if k < 4 else jnp.logical_not(low)

            @pl.when(slot < 2)
            def _():
                kept_ref[slot] = jnp.where(keep, total, kept_ref[slot])

            @pl.when(slot >= 2)
            def _():
                sent_ref[slot - 2] = jnp.where(keep, total, sent_ref[slot - 2])


def exchange(kept, sent):
    size = lax.axis_size("rows")
    cols = lax.axis_size("cols")

    def rows(x, bit):
        return lax.ppermute(x, "rows", [(i, i ^ bit) for i in range(size)])

    kept = kept + rows(sent, 1)
    kept = kept[0] + rows(kept[1], 2)
    bit = 4
    while bit < size:
        kept = kept + rows(kept, bit)
        bit *= 2
    bit = 1
    while bit < cols:
        kept = kept + lax.ppermute(kept, "cols", [(i, i ^ bit) for i in range(cols)])
        bit *= 2
    other = rows(kept, 2)
    return kept, other, rows(kept, 1), rows(other, 1)


def main_kernel(
    width, order, cells, mask, cell_ref, value_ref, var_ref, prior_ref, p0, p1, p2, p3,
    out_ref, first_ref, second_ref, predicted, table,
):
    height, cols = prior_ref.shape[0], prior_ref.shape[1]
    my_row, my_col = lax.axis_index("rows"), lax.axis_index("cols")
    across = width // cols
    my_tile = my_row * across + my_col
    mine = 2 * lax.rem(my_row, 2) + lax.rem(lax.div(my_row, 2), 2)
    for rel, part in enumerate((p0, p1, p2, p3)):
        predicted[jnp.bitwise_xor(rel, mine)] = part[...]
    low = low_lanes((cols, 2 * MEMBERS))
    for j in range(height // 2):
        for p in range(SPECIES // 2):
            a = prior_ref[2 * j, :, 128 * p : 128 * (p + 1)]
            b = prior_ref[2 * j + 1, :, 128 * p : 128 * (p + 1)]
            out_ref[j, 2 * p * cols : (2 * p + 1) * cols] = jnp.where(low, a, swap_halves(b))
            out_ref[j, (2 * p + 1) * cols : (2 * p + 2) * cols] = jnp.where(low, swap_halves(a), b)
    batches = [order[k] for k in range(BATCHES)]
    tiles = []
    for k in range(BATCHES):
        first = cells[batches[k], 0]
        tiles.append(lax.div(first, width * height) * across + lax.div(lax.rem(first, width), cols))
        table[k : k + 1, :] = cell_ref[pl.ds(batches[k], 1), :].astype(F32)
        table[8 + k : 9 + k, :] = value_ref[pl.ds(batches[k], 1), :]
        table[16 + k : 17 + k, :] = var_ref[pl.ds(batches[k], 1), :]
    cell_lane = table[0:8, :]
    row_lane = jnp.floor(cell_lane * (1.0 / width))
    col_lane = (cell_lane - row_lane * width) * (1.0 / HALFW)
    row_lane = row_lane * (1.0 / HALFW)
    row_col = jnp.transpose(row_lane)
    col_col = jnp.transpose(col_lane)
    value_col = jnp.transpose(table[8:16, :])
    var_col = jnp.transpose(table[16:24, :])
    low_obs = low_lanes((OBS, 2 * MEMBERS))
    x_pos = (my_col * cols + lax.broadcasted_iota(jnp.int32, (cols, OBS), 0)).astype(F32) * (
        1.0 / HALFW
    )

    def update(x, taper, spread_w, gain_w, gain_hi):
        high, low_part = split(x)
        c_high, c_low = split(dot(jnp.concatenate([high, low_part, high], 1), spread_w) * taper)
        both = dot(c_high, gain_w)
        return x + (both[:, : 2 * MEMBERS] + both[:, 2 * MEMBERS :] + dot(c_low, gain_hi))

    for k in range(BATCHES):
        block = predicted[k % 4]
        if k < 4:
            here = jnp.where(low_obs, block, swap_halves(block))
        else:
            here = jnp.where(low_obs, swap_halves(block), block)
        mean = jnp.sum(here, axis=1, keepdims=True) * (0.5 / MEMBERS)
        spread = here - mean
        variance = jnp.sum(spread * spread, axis=1, keepdims=True) * (0.5 / (MEMBERS - 1))
        var = var_col[:, k : k + 1]
        denominator = variance + var
        shrink = 1.0 / (1.0 + jnp.sqrt(var / denominator))
        gain = ((value_col[:, k : k + 1] - mean) - shrink * spread) / (
            denominator * (MEMBERS - 1)
        )
        turned = jnp.transpose(spread)
        top = lax.broadcasted_iota(jnp.int32, turned.shape, 0) < MEMBERS
        zero = jnp.zeros_like(turned)
        wide = jnp.concatenate([jnp.where(top, turned, zero), jnp.where(top, zero, turned)], 1)
        wide_hi, wide_lo = split(wide)
        spread_w = jnp.concatenate([wide_hi, wide_hi, wide_lo], 0)
        tall = jnp.concatenate([jnp.where(low_obs, gain, zero), jnp.where(low_obs, zero, gain)], 0)
        tall_hi, tall_lo = split(tall)
        gain_w = jnp.concatenate([tall_hi, tall_lo], 1)
        obs_row, obs_col = row_lane[k : k + 1, :], col_lane[k : k + 1, :]
        if k < BATCHES - 1:
            for q in range(4):
                if q + 4 <= k:
                    continue
                halves = []
                for later in (q, q + 4):
                    dr = row_col[:, later : later + 1] - obs_row
                    dc = col_col[:, later : later + 1] - obs_col
                    active = (mask[batches[k], tiles[later]] > 0).astype(F32)
                    halves.append(taper_weights(dr * dr + dc * dc) * active)
                predicted[q] = update(
                    predicted[q], jnp.concatenate(halves, 1), spread_w, gain_w, tall_hi
                )

        active = (mask[batches[k], my_tile] > 0).astype(F32)
        dx = x_pos - obs_col
        dx = dx * dx
        for j in range(height // 2):
            halves = []
            for h in range(2):
                dy = (my_row * height + 2 * j + h).astype(F32) * (1.0 / HALFW) - obs_row
                halves.append(taper_weights(dx + dy * dy) * active)
            taper = jnp.concatenate([jnp.concatenate(halves, 1)] * SPECIES, 0)
            out_ref[j] = update(out_ref[j], taper, spread_w, gain_w, tall_hi)

    even = lax.rem(my_col, 2) == 0
    for j in range(height // 2):
        for e in range(HALO):
            for t in range(SPECIES):
                r = t * cols + e
                a = out_ref[j, r : r + 1, :]
                r = t * cols + cols - HALO + e
                b = out_ref[j, r : r + 1, :]
                first_ref[j, e, t : t + 1, :] = jnp.where(even, b, a)
                second_ref[j, e, t : t + 1, :] = jnp.where(even, a, b)


def smooth_kernel(
    kern, mix, tile_ref, side0_ref, side1_ref, rows0_ref, rows1_ref, out_ref, padded, lines
):
    pairs, cols = tile_ref.shape[0], tile_ref.shape[1] // SPECIES
    depth = cols + 16
    lanes = 2 * MEMBERS
    even_row = lax.rem(lax.axis_index("rows"), 2) == 0
    even_col = lax.rem(lax.axis_index("cols"), 2) == 0
    edge = jnp.zeros((8, lanes), F32)

    for q in range(pairs + 4):
        inside = 2 <= q < pairs + 2
        p = q - 2 if inside else (q if q < 2 else q - pairs - 2)

        def outside(lo, hi):
            a, b = rows0_ref[p, lo:hi, :], rows1_ref[p, lo:hi, :]
            return jnp.where(even_row, b, a) if q < 2 else jnp.where(even_row, a, b)

        for t in range(SPECIES):
            padded[q, t, 0:8, :] = edge
            padded[q, t, depth - 8 : depth, :] = edge
            lo, hi = t * cols, (t + 1) * cols
            padded[q, t, 8 : 8 + cols, :] = tile_ref[p, lo:hi, :] if inside else outside(lo, hi)
            for e in range(HALO):
                if inside:
                    a, b = side0_ref[p, e, t : t + 1, :], side1_ref[p, e, t : t + 1, :]
                else:
                    at = SPECIES * cols + e * SPECIES + t
                    a = outside(at, at + 1)
                    b = outside(at + HALO * SPECIES, at + HALO * SPECIES + 1)
                padded[q, t, 5 + e : 6 + e, :] = jnp.where(even_col, b, a)
                padded[q, t, 8 + cols + e : 9 + cols + e, :] = jnp.where(even_col, a, b)
    column = lax.broadcasted_iota(jnp.int32, (cols, 3 * depth), 1)
    third = column >= 2 * depth
    column = jnp.where(third, column - 2 * depth, jnp.where(column >= depth, column - depth, column))
    offset = column - (lax.broadcasted_iota(jnp.int32, (cols, 3 * depth), 0) + 5)
    low = low_lanes((cols, lanes))

    def species(t, carry):
        bands = []
        for a in range(KW):
            band = jnp.zeros((cols, 3 * depth), F32)
            for e in range(KW):
                band = jnp.where(offset == e, kern[t, a * KW + e], band)
            high = band.astype(BF16).astype(F32)
            bands.append(jnp.where(third, band - high, high).astype(BF16))
        band = jnp.concatenate(bands, 0)
        for d in range(0, pairs + 4, 2):
            hi, lo = split(jnp.concatenate([padded[d, t], padded[d + 1, t]], 1))
            product = dot(band, jnp.concatenate([hi, lo, hi], 0))
            lines[d] = product[:, :lanes]
            lines[d + 1] = product[:, lanes:]

        def part(q, a):
            return lines[q, a * cols : (a + 1) * cols, :]

        def odd(u):
            return swap_halves(part(u, 0) + part(u + 1, 2) + part(u + 2, 4) + part(u + 3, 6))

        before = odd(0)
        for j in range(pairs):
            after = odd(j + 1)
            straight = part(j + 1, 1) + part(j + 2, 3) + part(j + 3, 5)
            padded[j, t, 0:cols, :] = straight + jnp.where(low, before, after)
            before = after
        return carry

    lax.fori_loop(0, SPECIES, species, 0)

    def mixed(j, carry):
        smooth = [padded[j, t, 0:cols, :] for t in range(SPECIES)]
        for p in range(SPECIES // 2):
            total = []
            for s in (2 * p, 2 * p + 1):
                acc = mix[s, 0] * smooth[0]
                for t in range(1, SPECIES):
                    acc = acc + mix[s, t] * smooth[t]
                total.append(acc)
            out_ref[2 * j, :, 128 * p : 128 * (p + 1)] = jnp.where(low, total[0], swap_halves(total[1]))
            out_ref[2 * j + 1, :, 128 * p : 128 * (p + 1)] = jnp.where(
                low, swap_halves(total[0]), total[1]
            )
        return carry

    lax.fori_loop(0, pairs, mixed, 0)


def shards(prior, obs_cell, obs_weight, obs_value, obs_var, loc_mask, batch_order, kernel, mixing):
    height, cols, channels = prior.shape
    across = lax.axis_size("cols")
    width = cols * across
    pairs = height // 2
    lanes = 2 * MEMBERS
    kept, sent = pl.pallas_call(
        functools.partial(gather_kernel, width),
        out_shape=(jax.ShapeDtypeStruct((2, OBS, lanes), F32),) * 2,
        in_specs=[SMEM, SMEM, VMEM, VMEM],
        out_specs=(VMEM, VMEM),
        scratch_shapes=[pltpu.VMEM((OBS, channels), F32)],
        compiler_params=PARAMS,
        name="gather",
    )(batch_order, obs_cell, jnp.transpose(obs_weight, (0, 2, 1)), prior)
    arrived = exchange(kept, sent)
    tile, first, second = pl.pallas_call(
        functools.partial(main_kernel, width),
        out_shape=(
            jax.ShapeDtypeStruct((pairs, SPECIES * cols, lanes), F32),
            jax.ShapeDtypeStruct((pairs, HALO, SPECIES, lanes), F32),
            jax.ShapeDtypeStruct((pairs, HALO, SPECIES, lanes), F32),
        ),
        in_specs=[SMEM] * 3 + [VMEM] * 8,
        out_specs=(VMEM, VMEM, VMEM),
        scratch_shapes=[pltpu.VMEM((4, OBS, lanes), F32), pltpu.VMEM((24, OBS), F32)],
        compiler_params=PARAMS,
        name="assimilate",
    )(batch_order, obs_cell, loc_mask, obs_cell, obs_value, obs_var, prior, *arrived)

    def swap(x, axis, start):
        size = lax.axis_size(axis)
        pairs_of = [(i, i + 1) for i in range(start, size - 1, 2)]
        return lax.ppermute(x, axis, pairs_of + [(j, i) for i, j in pairs_of])

    side0, side1 = swap(first, "cols", 0), swap(second, "cols", 1)

    def with_sides(lo, hi):
        flat = (hi - lo, HALO * SPECIES, lanes)
        return jnp.concatenate(
            [tile[lo:hi], side0[lo:hi].reshape(flat), side1[lo:hi].reshape(flat)], 1
        )

    even = lax.rem(lax.axis_index("rows"), 2) == 0
    bottom, top = with_sides(pairs - 2, pairs), with_sides(0, 2)
    rows0 = swap(jnp.where(even, bottom, top), "rows", 0)
    rows1 = swap(jnp.where(even, top, bottom), "rows", 1)
    return pl.pallas_call(
        smooth_kernel,
        out_shape=jax.ShapeDtypeStruct((height, cols, channels), F32),
        in_specs=[SMEM, SMEM] + [VMEM] * 5,
        out_specs=VMEM,
        scratch_shapes=[
            pltpu.VMEM((pairs + 4, SPECIES, cols + 16, lanes), F32),
            pltpu.VMEM((pairs + 4, KW * cols, lanes), F32),
        ],
        compiler_params=PARAMS,
        name="smooth",
    )(kernel.reshape(SPECIES, KW * KW), mixing, tile, side0, side1, rows0, rows1)


def solution(mesh):
    return jax.shard_map(
        shards,
        mesh=mesh,
        in_specs=(P("rows", "cols", None), P(), P(), P(), P(), P(), P(), P(), P()),
        out_specs=P("rows", "cols", None),
        check_vma=False,
    )
```

```python
import functools

import jax
import jax.numpy as jnp
from jax import lax
from jax.experimental import pallas as pl
from jax.experimental.pallas import tpu as pltpu
from jax.sharding import PartitionSpec as P

BATCHES = 8
OBS = 128
SPECIES = 8
MEMBERS = 64
KW = 7
HALO = KW // 2
HALFW = 48
BF16 = jnp.bfloat16
F32 = jnp.float32
VMEM = pl.BlockSpec(memory_space=pltpu.VMEM)
SMEM = pl.BlockSpec(memory_space=pltpu.SMEM)
PARAMS = pltpu.CompilerParams(vmem_limit_bytes=56 << 20)


def split(x):
    high = x.astype(BF16)
    return high, (x - high.astype(F32)).astype(BF16)


def dot(a, b):
    return jnp.dot(a, b, preferred_element_type=F32)


def swap_halves(x):
    return pltpu.roll(x, MEMBERS, axis=x.ndim - 1)


def low_lanes(shape):
    return lax.broadcasted_iota(jnp.int32, shape, len(shape) - 1) < MEMBERS


def taper_weights(squared):
    inverse = lax.rsqrt(jnp.maximum(squared, 1e-4))
    ratio = squared * inverse
    inner = 1.0 - (ratio * ratio) * (5.0 / 3.0 - ratio * (0.625 + ratio * (0.5 - 0.25 * ratio)))
    left = jnp.maximum(2.0 - ratio, 0.0)
    left = left * left
    outer = (left * left) * (((ratio + 2.0) * ratio - 0.5) * (inverse * (1.0 / 12.0)))
    return jnp.where(ratio <= 1.0, inner, outer)


def gather_kernel(width, order, cells, weight_ref, prior_ref, kept_ref, sent_ref, picked):
    height, cols = prior_ref.shape[0], prior_ref.shape[1]
    my_row, my_col = lax.axis_index("rows"), lax.axis_index("cols")
    mine = 2 * lax.rem(my_row, 2) + lax.rem(lax.div(my_row, 2), 2)
    kept_ref[...] = jnp.zeros_like(kept_ref)
    sent_ref[...] = jnp.zeros_like(sent_ref)
    for k in range(BATCHES):
        batch = order[k]
        first = cells[batch, 0]
        owner = (lax.div(first, width * height) == my_row) & (
            lax.div(lax.rem(first, width), cols) == my_col
        )

        @pl.when(owner)
        def _():
            def one(i, carry):
                cell = cells[batch, i]
                row = lax.div(cell, width) - my_row * height
                col = lax.rem(cell, width) - my_col * cols
                picked[pl.ds(i, 1), :] = prior_ref[row, pl.ds(col, 1), :]
                return carry

            lax.fori_loop(0, OBS, one, 0, unroll=8)
            weights = jnp.transpose(weight_ref[batch])
            low = low_lanes((OBS, 2 * MEMBERS))
            total = jnp.zeros((OBS, 2 * MEMBERS), F32)
            for p in range(SPECIES // 2):
                scale = jnp.where(low, weights[:, 2 * p : 2 * p + 1], weights[:, 2 * p + 1 : 2 * p + 2])
                total = total + scale * picked[:, 128 * p : 128 * (p + 1)]
            total = total + swap_halves(total)
            slot = jnp.bitwise_xor(k % 4, mine)
            keep = low if k < 4 else jnp.logical_not(low)

            @pl.when(slot < 2)
            def _():
                kept_ref[slot] = jnp.where(keep, total, kept_ref[slot])

            @pl.when(slot >= 2)
            def _():
                sent_ref[slot - 2] = jnp.where(keep, total, sent_ref[slot - 2])


def exchange(kept, sent):
    size = lax.axis_size("rows")
    cols = lax.axis_size("cols")

    def rows(x, bit):
        return lax.ppermute(x, "rows", [(i, i ^ bit) for i in range(size)])

    kept = kept + rows(sent, 1)
    kept = kept[0] + rows(kept[1], 2)
    bit = 4
    while bit < size:
        kept = kept + rows(kept, bit)
        bit *= 2
    bit = 1
    while bit < cols:
        kept = kept + lax.ppermute(kept, "cols", [(i, i ^ bit) for i in range(cols)])
        bit *= 2
    other = rows(kept, 2)
    return kept, other, rows(kept, 1), rows(other, 1)


def update(x, taper, spread_w, gain_w):
    high, low_part = split(x)
    c_high, c_low = split(dot(jnp.concatenate([high, low_part, high], 1), spread_w) * taper)
    both = dot(c_high, gain_w)
    lanes = 2 * MEMBERS
    return x + (both[:, :lanes] + both[:, lanes:] + dot(c_low, gain_w[:, :lanes]))


def load_pair(prior_ref, row, pair, lo, hi):
    low = low_lanes((hi - lo, 2 * MEMBERS))
    a = prior_ref[row, lo:hi, 128 * pair : 128 * (pair + 1)]
    b = prior_ref[row + 1, lo:hi, 128 * pair : 128 * (pair + 1)]
    return jnp.where(low, a, swap_halves(b)), jnp.where(low, swap_halves(a), b)


def positions(start, length):
    steps = lax.broadcasted_iota(jnp.int32, (length, OBS), 0)
    return (start + steps).astype(F32) * (1.0 / HALFW)


def pair_taper(first_row, gap, obs_row, active):
    halves = []
    for h in range(2):
        dy = (first_row + h).astype(F32) * (1.0 / HALFW) - obs_row
        halves.append(taper_weights(gap + dy * dy) * active)
    return jnp.concatenate(halves, 1)


def edge_kernel(
    width, order, cells, mask, cell_ref, value_ref, var_ref, prior_ref, p0, p1, p2, p3,
    rows_ref, ends_ref, send0_ref, send1_ref, first_ref, second_ref, spread_ref, gain_ref,
    place_ref, predicted, table,
):
    height, cols = prior_ref.shape[0], prior_ref.shape[1]
    my_row, my_col = lax.axis_index("rows"), lax.axis_index("cols")
    across = width // cols
    my_tile = my_row * across + my_col
    mine = 2 * lax.rem(my_row, 2) + lax.rem(lax.div(my_row, 2), 2)
    for rel, part in enumerate((p0, p1, p2, p3)):
        predicted[jnp.bitwise_xor(rel, mine)] = part[...]
    pairs = height // 2
    outer = (0, 1, pairs - 2, pairs - 1)
    inner = tuple(range(2, pairs - 2))
    for p in range(SPECIES // 2):
        for i, j in enumerate(outer):
            a, b = load_pair(prior_ref, 2 * j, p, 0, cols)
            rows_ref[i, 2 * p * cols : (2 * p + 1) * cols] = a
            rows_ref[i, (2 * p + 1) * cols : (2 * p + 2) * cols] = b
        for i, j in enumerate(inner):
            for side, lo in enumerate((0, cols - 8)):
                a, b = load_pair(prior_ref, 2 * j, p, lo, lo + 8)
                ends_ref[i, 2 * p, 8 * side : 8 * side + 8] = a
                ends_ref[i, 2 * p + 1, 8 * side : 8 * side + 8] = b
    batches = [order[k] for k in range(BATCHES)]
    tiles = []
    for k in range(BATCHES):
        first = cells[batches[k], 0]
        tiles.append(lax.div(first, width * height) * across + lax.div(lax.rem(first, width), cols))
        table[k : k + 1, :] = cell_ref[pl.ds(batches[k], 1), :].astype(F32)
        table[8 + k : 9 + k, :] = value_ref[pl.ds(batches[k], 1), :]
        table[16 + k : 17 + k, :] = var_ref[pl.ds(batches[k], 1), :]
    cell_lane = table[0:8, :]
    row_lane = jnp.floor(cell_lane * (1.0 / width))
    col_lane = (cell_lane - row_lane * width) * (1.0 / HALFW)
    row_lane = row_lane * (1.0 / HALFW)
    place_ref[0:8, :] = row_lane
    place_ref[8:16, :] = col_lane
    row_col = jnp.transpose(row_lane)
    col_col = jnp.transpose(col_lane)
    value_col = jnp.transpose(table[8:16, :])
    var_col = jnp.transpose(table[16:24, :])
    low_obs = low_lanes((OBS, 2 * MEMBERS))
    x_pos = positions(my_col * cols, cols)

    for k in range(BATCHES):
        block = predicted[k % 4]
        if k < 4:
            here = jnp.where(low_obs, block, swap_halves(block))
        else:
            here = jnp.where(low_obs, swap_halves(block), block)
        mean = jnp.sum(here, axis=1, keepdims=True) * (0.5 / MEMBERS)
        spread = here - mean
        variance = jnp.sum(spread * spread, axis=1, keepdims=True) * (0.5 / (MEMBERS - 1))
        var = var_col[:, k : k + 1]
        denominator = variance + var
        shrink = 1.0 / (1.0 + jnp.sqrt(var / denominator))
        gain = ((value_col[:, k : k + 1] - mean) - shrink * spread) / (
            denominator * (MEMBERS - 1)
        )
        turned = jnp.transpose(spread)
        top = lax.broadcasted_iota(jnp.int32, turned.shape, 0) < MEMBERS
        zero = jnp.zeros_like(turned)
        wide = jnp.concatenate([jnp.where(top, turned, zero), jnp.where(top, zero, turned)], 1)
        wide_hi, wide_lo = split(wide)
        spread_w = jnp.concatenate([wide_hi, wide_hi, wide_lo], 0)
        tall = jnp.concatenate([jnp.where(low_obs, gain, zero), jnp.where(low_obs, zero, gain)], 0)
        gain_w = jnp.concatenate(split(tall), 1)
        spread_ref[k] = spread_w
        gain_ref[k] = gain_w
        obs_row, obs_col = row_lane[k : k + 1, :], col_lane[k : k + 1, :]
        if k < BATCHES - 1:
            for q in range(4):
                if q + 4 <= k:
                    continue
                halves = []
                for later in (q, q + 4):
                    dr = row_col[:, later : later + 1] - obs_row
                    dc = col_col[:, later : later + 1] - obs_col
                    active = (mask[batches[k], tiles[later]] > 0).astype(F32)
                    halves.append(taper_weights(dr * dr + dc * dc) * active)
                predicted[q] = update(predicted[q], jnp.concatenate(halves, 1), spread_w, gain_w)
        active = (mask[batches[k], my_tile] > 0).astype(F32)
        gap = x_pos - obs_col
        gap = gap * gap
        for i, j in enumerate(outer):
            taper = pair_taper(my_row * height + 2 * j, gap, obs_row, active)
            rows_ref[i] = update(
                rows_ref[i], jnp.concatenate([taper] * SPECIES, 0), spread_w, gain_w
            )
        gap = jnp.concatenate([gap[:8], gap[cols - 8 :]], 0)
        tapers = []
        for j in inner:
            tapers += [pair_taper(my_row * height + 2 * j, gap, obs_row, active)] * SPECIES
        flat = (len(inner) * SPECIES * 16, 2 * MEMBERS)
        ends = update(ends_ref[...].reshape(flat), jnp.concatenate(tapers, 0), spread_w, gain_w)
        ends_ref[...] = ends.reshape(ends_ref.shape)

    even = lax.rem(my_row, 2) == 0
    low = low_lanes((cols, 2 * MEMBERS))
    for t in range(SPECIES):
        lo, hi = t * cols, (t + 1) * cols
        top, bottom = rows_ref[0, lo:hi, :], rows_ref[3, lo:hi, :]
        send0_ref[lo:hi, :] = jnp.where(even, bottom, top)
        send1_ref[lo:hi, :] = jnp.where(even, top, bottom)
    base = SPECIES * cols
    for p in range(SPECIES // 2):
        a, b = slice(2 * p * cols, (2 * p + 1) * cols), slice((2 * p + 1) * cols, (2 * p + 2) * cols)
        top = jnp.where(low, rows_ref[1, a, :], swap_halves(rows_ref[1, b, :]))
        bottom = jnp.where(low, swap_halves(rows_ref[2, a, :]), rows_ref[2, b, :])
        lo, hi = base + p * cols, base + (p + 1) * cols
        send0_ref[lo:hi, :] = jnp.where(even, bottom, top)
        send1_ref[lo:hi, :] = jnp.where(even, top, bottom)
    even = lax.rem(my_col, 2) == 0
    for j in range(pairs):
        for t in range(SPECIES):
            if j in outer:
                i = outer.index(j)
                a = rows_ref[i, t * cols : t * cols + HALO, :]
                b = rows_ref[i, (t + 1) * cols - HALO : (t + 1) * cols, :]
            else:
                a = ends_ref[j - 2, t, 0:HALO, :]
                b = ends_ref[j - 2, t, 16 - HALO : 16, :]
            first_ref[j * SPECIES + t] = jnp.where(even, b, a)
            second_ref[j * SPECIES + t] = jnp.where(even, a, b)


def inner_kernel(first_row, height, order, mask, prior_ref, spread_ref, gain_ref, place_ref, out_ref):
    cols = prior_ref.shape[1]
    across = lax.axis_size("cols")
    my_row, my_col = lax.axis_index("rows"), lax.axis_index("cols")
    my_tile = my_row * across + my_col
    pairs = out_ref.shape[0]
    for j in range(pairs):
        for p in range(SPECIES // 2):
            a, b = load_pair(prior_ref, 2 * j, p, 8, cols - 8)
            out_ref[j, 2 * p] = a
            out_ref[j, 2 * p + 1] = b
    x_pos = positions(my_col * cols + 8, cols - 16)
    flat = (SPECIES * (cols - 16), 2 * MEMBERS)
    for k in range(BATCHES):
        active = (mask[order[k], my_tile] > 0).astype(F32)
        obs_row = place_ref[k : k + 1, :]
        gap = x_pos - place_ref[8 + k : 9 + k, :]
        gap = gap * gap
        spread_w, gain_w = spread_ref[k], gain_ref[k]
        for j in range(pairs):
            taper = pair_taper(my_row * height + first_row + 2 * j, gap, obs_row, active)
            taper = jnp.concatenate([taper] * SPECIES, 0)
            new = update(out_ref[j].reshape(flat), taper, spread_w, gain_w)
            out_ref[j] = new.reshape(SPECIES, cols - 16, 2 * MEMBERS)


def smooth_kernel(
    kern, mix, rows_ref, ends_ref, mid0_ref, mid1_ref, side0_ref, side1_ref, rows0_ref, rows1_ref,
    out_ref, padded, lines,
):
    cols = mid0_ref.shape[2] + 16
    inner = ends_ref.shape[0]
    pairs = inner + 4
    depth = cols + 16
    lanes = 2 * MEMBERS
    even_row = lax.rem(lax.axis_index("rows"), 2) == 0
    even_col = lax.rem(lax.axis_index("cols"), 2) == 0
    edge = jnp.zeros((8, lanes), F32)
    own = pairs * SPECIES
    packed = SPECIES + SPECIES // 2
    above = jnp.where(even_row, own + packed, own)
    below = jnp.where(even_row, own, own + packed)

    for q in range(pairs + 4):
        p = q - 2
        for t in range(SPECIES):
            padded[q, t, 0:8, :] = edge
            padded[q, t, depth - 8 : depth, :] = edge
            if 0 <= p < pairs:
                at = p * SPECIES + t
                if p < 2 or p >= pairs - 2:
                    i = p if p < 2 else p - pairs + 4
                    padded[q, t, 8 : 8 + cols, :] = rows_ref[i, t * cols : (t + 1) * cols, :]
                else:
                    i = p - 2
                    mid = mid0_ref if i < inner // 2 else mid1_ref
                    padded[q, t, 8:16, :] = ends_ref[i, t, 0:8, :]
                    padded[q, t, 16:cols, :] = mid[i % (inner // 2), t]
                    padded[q, t, cols : cols + 8, :] = ends_ref[i, t, 8:16, :]

                def unpack(x):
                    return x

            else:
                base = above if q < 2 else below
                whole = q in (1, pairs + 2)
                at = base + t if whole else base + SPECIES + t // 2
                lo = t * cols if whole else (SPECIES + t // 2) * cols
                a, b = rows0_ref[lo : lo + cols, :], rows1_ref[lo : lo + cols, :]
                body = jnp.where(even_row, b, a) if q < 2 else jnp.where(even_row, a, b)

                def unpack(x):
                    wanted = 1 if q < 2 else 0
                    return x if whole or t % 2 == wanted else swap_halves(x)

                padded[q, t, 8 : 8 + cols, :] = unpack(body)
            a, b = side0_ref[at], side1_ref[at]
            padded[q, t, 5:8, :] = unpack(jnp.where(even_col, b, a))
            padded[q, t, 8 + cols : 11 + cols, :] = unpack(jnp.where(even_col, a, b))
    column = lax.broadcasted_iota(jnp.int32, (cols, 3 * depth), 1)
    third = column >= 2 * depth
    column = jnp.where(third, column - 2 * depth, jnp.where(column >= depth, column - depth, column))
    offset = column - (lax.broadcasted_iota(jnp.int32, (cols, 3 * depth), 0) + 5)
    low = low_lanes((cols, lanes))

    def species(t, carry):
        bands = []
        for a in range(KW):
            band = jnp.zeros((cols, 3 * depth), F32)
            for e in range(KW):
                band = jnp.where(offset == e, kern[t, a * KW + e], band)
            high = band.astype(BF16).astype(F32)
            bands.append(jnp.where(third, band - high, high).astype(BF16))
        band = jnp.concatenate(bands, 0)
        for d in range(0, pairs + 4, 2):
            hi, lo = split(jnp.concatenate([padded[d, t], padded[d + 1, t]], 1))
            product = dot(band, jnp.concatenate([hi, lo, hi], 0))
            lines[d] = product[:, :lanes]
            lines[d + 1] = product[:, lanes:]

        def part(q, a):
            return lines[q, a * cols : (a + 1) * cols, :]

        def odd(u):
            return swap_halves(part(u, 0) + part(u + 1, 2) + part(u + 2, 4) + part(u + 3, 6))

        before = odd(0)
        for j in range(pairs):
            after = odd(j + 1)
            straight = part(j + 1, 1) + part(j + 2, 3) + part(j + 3, 5)
            padded[j, t, 0:cols, :] = straight + jnp.where(low, before, after)
            before = after
        return carry

    lax.fori_loop(0, SPECIES, species, 0)

    def mixed(j, carry):
        smooth = [padded[j, t, 0:cols, :] for t in range(SPECIES)]
        for p in range(SPECIES // 2):
            total = []
            for s in (2 * p, 2 * p + 1):
                acc = mix[s, 0] * smooth[0]
                for t in range(1, SPECIES):
                    acc = acc + mix[s, t] * smooth[t]
                total.append(acc)
            out_ref[2 * j, :, 128 * p : 128 * (p + 1)] = jnp.where(low, total[0], swap_halves(total[1]))
            out_ref[2 * j + 1, :, 128 * p : 128 * (p + 1)] = jnp.where(
                low, swap_halves(total[0]), total[1]
            )
        return carry

    lax.fori_loop(0, pairs, mixed, 0)


def shards(prior, obs_cell, obs_weight, obs_value, obs_var, loc_mask, batch_order, kernel, mixing):
    height, cols, channels = prior.shape
    across = lax.axis_size("cols")
    width = cols * across
    pairs = height // 2
    lanes = 2 * MEMBERS
    kept, sent = pl.pallas_call(
        functools.partial(gather_kernel, width),
        out_shape=(jax.ShapeDtypeStruct((2, OBS, lanes), F32),) * 2,
        in_specs=[SMEM, SMEM, VMEM, VMEM],
        out_specs=(VMEM, VMEM),
        scratch_shapes=[pltpu.VMEM((OBS, channels), F32)],
        compiler_params=PARAMS,
        name="gather",
    )(batch_order, obs_cell, jnp.transpose(obs_weight, (0, 2, 1)), prior)
    arrived = exchange(kept, sent)
    inner = pairs - 4
    f32 = lambda *shape: jax.ShapeDtypeStruct(shape, F32)
    rows, ends, send0, send1, first, second, spread, gain, place = pl.pallas_call(
        functools.partial(edge_kernel, width),
        out_shape=(
            f32(4, SPECIES * cols, lanes),
            f32(inner, SPECIES, 16, lanes),
            f32((SPECIES + SPECIES // 2) * cols, lanes),
            f32((SPECIES + SPECIES // 2) * cols, lanes),
            f32(pairs * SPECIES, HALO, lanes),
            f32(pairs * SPECIES, HALO, lanes),
            jax.ShapeDtypeStruct((BATCHES, 3 * lanes, 2 * OBS), BF16),
            jax.ShapeDtypeStruct((BATCHES, 2 * OBS, 2 * lanes), BF16),
            f32(2 * BATCHES, OBS),
        ),
        in_specs=[SMEM] * 3 + [VMEM] * 8,
        out_specs=(VMEM,) * 9,
        scratch_shapes=[pltpu.VMEM((4, OBS, lanes), F32), pltpu.VMEM((24, OBS), F32)],
        compiler_params=PARAMS,
        name="edges",
    )(batch_order, obs_cell, loc_mask, obs_cell, obs_value, obs_var, prior, *arrived)

    def middle(part):
        count = inner // 2
        block = 2 * count
        index = 4 // block + part
        return pl.pallas_call(
            functools.partial(inner_kernel, 4 + block * part, height),
            out_shape=f32(count, SPECIES, cols - 16, lanes),
            grid=(1,),
            in_specs=[SMEM, SMEM, pl.BlockSpec((block, cols, channels), lambda i: (index, 0, 0))]
            + [VMEM] * 3,
            out_specs=VMEM,
            compiler_params=PARAMS,
            name="inner",
        )(batch_order, loc_mask, prior, spread, gain, place)

    def swap(x, axis, start):
        size = lax.axis_size(axis)
        pairs_of = [(i, i + 1) for i in range(start, size - 1, 2)]
        return lax.ppermute(x, axis, pairs_of + [(j, i) for i, j in pairs_of])

    rows1 = swap(send1, "rows", 1)
    rows0 = swap(send0, "rows", 0)
    mid0 = middle(0)
    rows0, rows1, mid0 = lax.optimization_barrier((rows0, rows1, mid0))
    even = lax.rem(lax.axis_index("cols"), 2) == 0

    def corner(x, at_right):
        strips = x.reshape(SPECIES + SPECIES // 2, cols, lanes)
        return jnp.where(at_right, strips[:, cols - HALO :], strips[:, :HALO])

    first = jnp.concatenate([first, corner(rows0, even), corner(rows1, even)], 0)
    odd = jnp.logical_not(even)
    second = jnp.concatenate([second, corner(rows0, odd), corner(rows1, odd)], 0)
    side1 = swap(second, "cols", 1)
    side0 = swap(first, "cols", 0)
    mid1 = middle(1)
    side0, side1, mid1 = lax.optimization_barrier((side0, side1, mid1))
    return pl.pallas_call(
        smooth_kernel,
        out_shape=jax.ShapeDtypeStruct((height, cols, channels), F32),
        in_specs=[SMEM, SMEM] + [VMEM] * 8,
        out_specs=VMEM,
        scratch_shapes=[
            pltpu.VMEM((pairs + 4, SPECIES, cols + 16, lanes), F32),
            pltpu.VMEM((pairs + 4, KW * cols, lanes), F32),
        ],
        compiler_params=PARAMS,
        name="smooth",
    )(kernel.reshape(SPECIES, KW * KW), mixing, rows, ends, mid0, mid1, side0, side1, rows0, rows1)


def solution(mesh):
    return jax.shard_map(
        shards,
        mesh=mesh,
        in_specs=(P("rows", "cols", None), P(), P(), P(), P(), P(), P(), P(), P()),
        out_specs=P("rows", "cols", None),
        check_vma=False,
    )
```

```python
import functools

import jax
import jax.numpy as jnp
from jax import lax
from jax.experimental import pallas as pl
from jax.experimental.pallas import tpu as pltpu
from jax.sharding import PartitionSpec as P

BATCHES = 8
OBS = 128
SPECIES = 8
MEMBERS = 64
KW = 7
HALO = KW // 2
HALFW = 48
BF16 = jnp.bfloat16
F32 = jnp.float32
VMEM = pl.BlockSpec(memory_space=pltpu.VMEM)
SMEM = pl.BlockSpec(memory_space=pltpu.SMEM)
PARAMS = pltpu.CompilerParams(vmem_limit_bytes=56 << 20)


def split(x):
    high = x.astype(BF16)
    return high, (x - high.astype(F32)).astype(BF16)


def dot(a, b):
    return jnp.dot(a, b, preferred_element_type=F32)


def swap_halves(x):
    return pltpu.roll(x, MEMBERS, axis=x.ndim - 1)


def low_lanes(shape):
    return lax.broadcasted_iota(jnp.int32, shape, len(shape) - 1) < MEMBERS


def taper_weights(squared):
    inverse = lax.rsqrt(jnp.maximum(squared, 1e-4))
    ratio = squared * inverse
    inner = 1.0 - (ratio * ratio) * (5.0 / 3.0 - ratio * (0.625 + ratio * (0.5 - 0.25 * ratio)))
    left = jnp.maximum(2.0 - ratio, 0.0)
    left = left * left
    outer = (left * left) * (((ratio + 2.0) * ratio - 0.5) * (inverse * (1.0 / 12.0)))
    return jnp.where(ratio <= 1.0, inner, outer)


def gather_kernel(width, order, cells, weight_ref, prior_ref, kept_ref, sent_ref, picked):
    height, cols = prior_ref.shape[0], prior_ref.shape[1]
    my_row, my_col = lax.axis_index("rows"), lax.axis_index("cols")
    mine = 2 * lax.rem(my_row, 2) + lax.rem(lax.div(my_row, 2), 2)
    corner = my_row * height * width + my_col * cols
    kept_ref[...] = jnp.zeros_like(kept_ref)
    sent_ref[...] = jnp.zeros_like(sent_ref)
    for k in range(BATCHES):
        batch = order[k]
        first = cells[batch, 0]
        owner = (lax.div(first, width * height) == my_row) & (
            lax.div(lax.rem(first, width), cols) == my_col
        )

        @pl.when(owner)
        def _():
            def one(i, carry):
                cell = cells[batch, i] - corner
                row = lax.div(cell, width)
                picked[pl.ds(i, 1), :] = prior_ref[row, pl.ds(cell - row * width, 1), :]
                return carry

            lax.fori_loop(0, OBS, one, 0, unroll=8)
            weights = jnp.transpose(weight_ref[batch])
            low = low_lanes((OBS, 2 * MEMBERS))
            total = jnp.zeros((OBS, 2 * MEMBERS), F32)
            for p in range(SPECIES // 2):
                scale = jnp.where(low, weights[:, 2 * p : 2 * p + 1], weights[:, 2 * p + 1 : 2 * p + 2])
                total = total + scale * picked[:, 128 * p : 128 * (p + 1)]
            total = total + swap_halves(total)
            slot = jnp.bitwise_xor(k % 4, mine)
            keep = low if k < 4 else jnp.logical_not(low)

            @pl.when(slot < 2)
            def _():
                kept_ref[slot] = jnp.where(keep, total, kept_ref[slot])

            @pl.when(slot >= 2)
            def _():
                sent_ref[slot - 2] = jnp.where(keep, total, sent_ref[slot - 2])


def exchange(kept, sent):
    size = lax.axis_size("rows")
    cols = lax.axis_size("cols")

    def rows(x, bit):
        return lax.ppermute(x, "rows", [(i, i ^ bit) for i in range(size)])

    kept = kept + rows(sent, 1)
    kept = kept[0] + rows(kept[1], 2)
    bit = 4
    while bit < size:
        kept = kept + rows(kept, bit)
        bit *= 2
    bit = 1
    while bit < cols:
        kept = kept + lax.ppermute(kept, "cols", [(i, i ^ bit) for i in range(cols)])
        bit *= 2
    other = rows(kept, 2)
    return kept, other, rows(kept, 1), rows(other, 1)


def update(x, taper, spread_w, gain_w):
    high, low_part = split(x)
    c_high, c_low = split(dot(jnp.concatenate([high, low_part, high], 1), spread_w) * taper)
    both = dot(c_high, gain_w)
    lanes = 2 * MEMBERS
    return x + (both[:, :lanes] + both[:, lanes:] + dot(c_low, gain_w[:, :lanes]))


def pair_up(a, b):
    low = low_lanes(a.shape)
    return jnp.where(low, a, swap_halves(b)), jnp.where(low, swap_halves(a), b)


def forecast_kernel(
    width, order, cells, mask, kern, mix, cell_ref, value_ref, var_ref, prior_ref,
    side0_ref, side1_ref, rows0_ref, rows1_ref, p0, p1, p2, p3,
    out_ref, field, predicted, table, lines,
):
    height, cols = prior_ref.shape[0], prior_ref.shape[1]
    my_row, my_col = lax.axis_index("rows"), lax.axis_index("cols")
    down, across = lax.axis_size("rows"), lax.axis_size("cols")
    mine = 2 * lax.rem(my_row, 2) + lax.rem(lax.div(my_row, 2), 2)
    for rel, part in enumerate((p0, p1, p2, p3)):
        predicted[jnp.bitwise_xor(rel, mine)] = part[...]
    pairs = height // 2
    depth = cols + 8
    lanes = 2 * MEMBERS
    even_row = lax.rem(my_row, 2) == 0
    even_col = lax.rem(my_col, 2) == 0

    def put(j, p, lo, a, b):
        first, second = pair_up(a, b)
        field[j, 2 * p, lo : lo + a.shape[0], :] = first
        field[j, 2 * p + 1, lo : lo + a.shape[0], :] = second

    for j in range(pairs + 3):
        for t in range(SPECIES):
            field[j, t, cols:depth, :] = jnp.zeros((8, lanes), F32)
    for p in range(SPECIES // 2):
        at = slice(128 * p, 128 * (p + 1))

        def left(r):
            return jnp.where(even_col, side1_ref[r, :, at], side0_ref[r, :, at])

        def right(r):
            return jnp.where(even_col, side0_ref[r, :, at], side1_ref[r, :, at])

        def above(r, lo, hi):
            return jnp.where(even_row, rows1_ref[r, lo:hi, at], rows0_ref[r, lo:hi, at])

        def below(r, lo, hi):
            return jnp.where(even_row, rows0_ref[r, lo:hi, at], rows1_ref[r, lo:hi, at])

        for j in range(pairs):
            put(j, p, 0, prior_ref[2 * j, :, at], prior_ref[2 * j + 1, :, at])
            put(j, p, cols, left(2 * j), left(2 * j + 1))
            put(j, p, cols + HALO, right(2 * j), right(2 * j + 1))
        for lo, hi in ((0, cols), (cols, cols + 2 * HALO)):
            put(pairs, p, lo, above(1, lo, hi), above(2, lo, hi))
            put(pairs + 1, p, lo, below(0, lo, hi), below(1, lo, hi))
            put(pairs + 2, p, lo, above(0, lo, hi), below(2, lo, hi))
    batches = [order[k] for k in range(BATCHES)]
    tiles = []
    for k in range(BATCHES):
        first = cells[batches[k], 0]
        tiles.append(lax.div(first, width * height) * across + lax.div(lax.rem(first, width), cols))
        table[k : k + 1, :] = cell_ref[pl.ds(batches[k], 1), :].astype(F32)
        table[8 + k : 9 + k, :] = value_ref[pl.ds(batches[k], 1), :]
        table[16 + k : 17 + k, :] = var_ref[pl.ds(batches[k], 1), :]
    cell_lane = table[0:8, :]
    row_lane = jnp.floor(cell_lane * (1.0 / width))
    col_lane = (cell_lane - row_lane * width) * (1.0 / HALFW)
    row_lane = row_lane * (1.0 / HALFW)
    row_col = jnp.transpose(row_lane)
    col_col = jnp.transpose(col_lane)
    value_col = jnp.transpose(table[8:16, :])
    var_col = jnp.transpose(table[16:24, :])
    low_obs = low_lanes((OBS, 2 * MEMBERS))
    index = lax.broadcasted_iota(jnp.int32, (depth, OBS), 0)
    to_left = (index >= cols) & (index < cols + HALO)
    to_right = index >= cols + HALO
    x_pos = jnp.where(to_left, index - cols - HALO, jnp.where(to_right, index - HALO, index))
    x_pos = (x_pos + my_col * cols).astype(F32) * (1.0 / HALFW)
    top_row = my_row * height
    zones = (
        jnp.maximum(my_row - 1, 0) * across, my_row * across, jnp.minimum(my_row + 1, down - 1) * across
    )
    sides = (jnp.maximum(my_col - 1, 0), my_col, jnp.minimum(my_col + 1, across - 1))
    row_pairs = [((top_row + 2 * j, 1), (top_row + 2 * j + 1, 1)) for j in range(pairs)]
    row_pairs += [
        ((top_row - 2, 0), (top_row - 1, 0)),
        ((top_row + height, 2), (top_row + height + 1, 2)),
        ((top_row - 3, 0), (top_row + height + 2, 2)),
    ]

    for k in range(BATCHES):
        block = predicted[k % 4]
        if k < 4:
            here = jnp.where(low_obs, block, swap_halves(block))
        else:
            here = jnp.where(low_obs, swap_halves(block), block)
        mean = jnp.sum(here, axis=1, keepdims=True) * (0.5 / MEMBERS)
        spread = here - mean
        variance = jnp.sum(spread * spread, axis=1, keepdims=True) * (0.5 / (MEMBERS - 1))
        var = var_col[:, k : k + 1]
        denominator = variance + var
        shrink = 1.0 / (1.0 + jnp.sqrt(var / denominator))
        gain = ((value_col[:, k : k + 1] - mean) - shrink * spread) / (
            denominator * (MEMBERS - 1)
        )
        turned = jnp.transpose(spread)
        top = lax.broadcasted_iota(jnp.int32, turned.shape, 0) < MEMBERS
        zero = jnp.zeros_like(turned)
        wide = jnp.concatenate([jnp.where(top, turned, zero), jnp.where(top, zero, turned)], 1)
        wide_hi, wide_lo = split(wide)
        spread_w = jnp.concatenate([wide_hi, wide_hi, wide_lo], 0)
        tall = jnp.concatenate([jnp.where(low_obs, gain, zero), jnp.where(low_obs, zero, gain)], 0)
        gain_w = jnp.concatenate(split(tall), 1)
        obs_row, obs_col = row_lane[k : k + 1, :], col_lane[k : k + 1, :]
        if k < BATCHES - 1:
            for q in range(4):
                if q + 4 <= k:
                    continue
                halves = []
                for later in (q, q + 4):
                    dr = row_col[:, later : later + 1] - obs_row
                    dc = col_col[:, later : later + 1] - obs_col
                    active = (mask[batches[k], tiles[later]] > 0).astype(F32)
                    halves.append(taper_weights(dr * dr + dc * dc) * active)
                predicted[q] = update(predicted[q], jnp.concatenate(halves, 1), spread_w, gain_w)
        gap = x_pos - obs_col
        gap = gap * gap
        active = []
        for zone in zones:
            on = [(mask[batches[k], zone + side] > 0).astype(F32) for side in sides]
            active.append(jnp.where(to_left, on[0], jnp.where(to_right, on[2], on[1])))
        flat = (SPECIES * depth, lanes)
        for j in range(pairs + 3):
            halves = []
            for position, zone in row_pairs[j]:
                dy = position.astype(F32) * (1.0 / HALFW) - obs_row
                halves.append(taper_weights(gap + dy * dy) * active[zone])
            taper = jnp.concatenate([jnp.concatenate(halves, 1)] * SPECIES, 0)
            new = update(field[j].reshape(flat), taper, spread_w, gain_w)
            field[j] = new.reshape(SPECIES, depth, lanes)

    sources = [pairs + 2, pairs] + list(range(pairs)) + [pairs + 1, pairs + 2]
    column = lax.broadcasted_iota(jnp.int32, (cols, 3 * depth), 1)
    third = column >= 2 * depth
    column = jnp.where(third, column - 2 * depth, jnp.where(column >= depth, column - depth, column))
    column = jnp.where(
        column < cols, column, jnp.where(column < cols + HALO, column - cols - HALO, column - HALO)
    )
    offset = column - lax.broadcasted_iota(jnp.int32, (cols, 3 * depth), 0) + HALO
    low = low_lanes((cols, lanes))

    def species(t, carry):
        bands = []
        for a in range(KW):
            band = jnp.zeros((cols, 3 * depth), F32)
            for e in range(KW):
                band = jnp.where(offset == e, kern[t, a * KW + e], band)
            high = band.astype(BF16).astype(F32)
            bands.append(jnp.where(third, band - high, high).astype(BF16))
        band = jnp.concatenate(bands, 0)
        for d in range(0, pairs + 4, 2):
            pieces = []
            for q in (d, d + 1):
                piece = field[sources[q], t]
                pieces.append(swap_halves(piece) if q in (0, pairs + 3) else piece)
            data = jnp.concatenate(pieces, 1)
            high = data.astype(BF16).astype(F32)
            data = jnp.concatenate([high, data - high, high], 0).astype(BF16)
            product = dot(band, data)
            lines[d] = product[:, :lanes]
            lines[d + 1] = product[:, lanes:]

        def part(q, a):
            return lines[q, a * cols : (a + 1) * cols, :]

        def odd(u):
            return swap_halves(part(u, 0) + part(u + 1, 2) + part(u + 2, 4) + part(u + 3, 6))

        before = odd(0)
        for j in range(pairs):
            after = odd(j + 1)
            straight = part(j + 1, 1) + part(j + 2, 3) + part(j + 3, 5)
            field[j, t, 0:cols, :] = straight + jnp.where(low, before, after)
            before = after
        return carry

    lax.fori_loop(0, SPECIES, species, 0)

    def mixed(j, carry):
        smooth = [field[j, t, 0:cols, :] for t in range(SPECIES)]
        for p in range(SPECIES // 2):
            total = []
            for s in (2 * p, 2 * p + 1):
                acc = mix[s, 0] * smooth[0]
                for t in range(1, SPECIES):
                    acc = acc + mix[s, t] * smooth[t]
                total.append(acc)
            out_ref[2 * j, :, 128 * p : 128 * (p + 1)] = jnp.where(low, total[0], swap_halves(total[1]))
            out_ref[2 * j + 1, :, 128 * p : 128 * (p + 1)] = jnp.where(
                low, swap_halves(total[0]), total[1]
            )
        return carry

    lax.fori_loop(0, pairs, mixed, 0)


def shards(prior, obs_cell, obs_weight, obs_value, obs_var, loc_mask, batch_order, kernel, mixing):
    height, cols, channels = prior.shape
    across = lax.axis_size("cols")
    width = cols * across
    pairs = height // 2
    lanes = 2 * MEMBERS
    kept, sent = pl.pallas_call(
        functools.partial(gather_kernel, width),
        out_shape=(jax.ShapeDtypeStruct((2, OBS, lanes), F32),) * 2,
        in_specs=[SMEM, SMEM, VMEM, VMEM],
        out_specs=(VMEM, VMEM),
        scratch_shapes=[pltpu.VMEM((OBS, channels), F32)],
        compiler_params=PARAMS,
        name="gather",
    )(batch_order, obs_cell, jnp.transpose(obs_weight, (0, 2, 1)), prior)
    arrived = exchange(kept, sent)

    def swap(x, axis, start):
        size = lax.axis_size(axis)
        pairs_of = [(i, i + 1) for i in range(start, size - 1, 2)]
        return lax.ppermute(x, axis, pairs_of + [(j, i) for i, j in pairs_of])

    even_row = lax.rem(lax.axis_index("rows"), 2) == 0
    even_col = lax.rem(lax.axis_index("cols"), 2) == 0
    first, last = prior[:, :HALO], prior[:, cols - HALO :]
    side1 = swap(jnp.where(even_col, first, last), "cols", 1)
    side0 = swap(jnp.where(even_col, last, first), "cols", 0)
    left = jnp.where(even_col, side1, side0)
    right = jnp.where(even_col, side0, side1)

    def strip(lo, hi):
        return jnp.concatenate([prior[lo:hi], left[lo:hi], right[lo:hi]], 1)

    top, bottom = strip(0, HALO), strip(height - HALO, height)
    rows1 = swap(jnp.where(even_row, top, bottom), "rows", 1)
    rows0 = swap(jnp.where(even_row, bottom, top), "rows", 0)
    return pl.pallas_call(
        functools.partial(forecast_kernel, width),
        out_shape=jax.ShapeDtypeStruct((height, cols, channels), F32),
        in_specs=[SMEM] * 5 + [VMEM] * 12,
        out_specs=VMEM,
        scratch_shapes=[
            pltpu.VMEM((pairs + 3, SPECIES, cols + 8, lanes), F32),
            pltpu.VMEM((4, OBS, lanes), F32),
            pltpu.VMEM((24, OBS), F32),
            pltpu.VMEM((pairs + 4, KW * cols, lanes), F32),
        ],
        compiler_params=PARAMS,
        name="forecast",
    )(
        batch_order, obs_cell, loc_mask, kernel.reshape(SPECIES, KW * KW), mixing,
        obs_cell, obs_value, obs_var, prior, side0, side1, rows0, rows1, *arrived,
    )


def solution(mesh):
    return jax.shard_map(
        shards,
        mesh=mesh,
        in_specs=(P("rows", "cols", None), P(), P(), P(), P(), P(), P(), P(), P()),
        out_specs=P("rows", "cols", None),
        check_vma=False,
    )
```

```python
import functools

import jax
import jax.numpy as jnp
from jax import lax
from jax.experimental import pallas as pl
from jax.experimental.pallas import tpu as pltpu
from jax.sharding import PartitionSpec as P

BATCHES = 8
OBS = 128
SPECIES = 8
MEMBERS = 64
KW = 7
HALO = KW // 2
HALFW = 48
BF16 = jnp.bfloat16
F32 = jnp.float32
VMEM = pl.BlockSpec(memory_space=pltpu.VMEM)
SMEM = pl.BlockSpec(memory_space=pltpu.SMEM)
PARAMS = pltpu.CompilerParams(vmem_limit_bytes=56 << 20)


def split(x):
    high = x.astype(BF16)
    return high, (x - high.astype(F32)).astype(BF16)


def dot(a, b):
    return jnp.dot(a, b, preferred_element_type=F32)


def swap_halves(x):
    return pltpu.roll(x, MEMBERS, axis=x.ndim - 1)


def low_lanes(shape):
    return lax.broadcasted_iota(jnp.int32, shape, len(shape) - 1) < MEMBERS


def taper_weights(squared):
    inverse = lax.rsqrt(jnp.maximum(squared, 1e-4))
    ratio = squared * inverse
    inner = 1.0 - (ratio * ratio) * (5.0 / 3.0 - ratio * (0.625 + ratio * (0.5 - 0.25 * ratio)))
    left = jnp.maximum(2.0 - ratio, 0.0)
    left = left * left
    outer = (left * left) * (((ratio + 2.0) * ratio - 0.5) * (inverse * (1.0 / 12.0)))
    return jnp.where(ratio <= 1.0, inner, outer)


def gather_kernel(width, order, cells, weight_ref, prior_ref, kept_ref, sent_ref, picked):
    height, cols = prior_ref.shape[0], prior_ref.shape[1]
    my_row, my_col = lax.axis_index("rows"), lax.axis_index("cols")
    mine = 2 * lax.rem(my_row, 2) + lax.rem(lax.div(my_row, 2), 2)
    corner = my_row * height * width + my_col * cols
    kept_ref[...] = jnp.zeros_like(kept_ref)
    sent_ref[...] = jnp.zeros_like(sent_ref)
    for k in range(BATCHES):
        batch = order[k]
        first = cells[batch, 0]
        owner = (lax.div(first, width * height) == my_row) & (
            lax.div(lax.rem(first, width), cols) == my_col
        )

        @pl.when(owner)
        def _():
            def one(i, carry):
                cell = cells[batch, i] - corner
                row = lax.div(cell, width)
                picked[pl.ds(i, 1), :] = prior_ref[row, pl.ds(cell - row * width, 1), :]
                return carry

            lax.fori_loop(0, OBS, one, 0, unroll=8)
            weights = jnp.transpose(weight_ref[batch])
            low = low_lanes((OBS, 2 * MEMBERS))
            total = jnp.zeros((OBS, 2 * MEMBERS), F32)
            for p in range(SPECIES // 2):
                scale = jnp.where(low, weights[:, 2 * p : 2 * p + 1], weights[:, 2 * p + 1 : 2 * p + 2])
                total = total + scale * picked[:, 128 * p : 128 * (p + 1)]
            total = total + swap_halves(total)
            slot = jnp.bitwise_xor(k % 4, mine)
            keep = low if k < 4 else jnp.logical_not(low)

            @pl.when(slot < 2)
            def _():
                kept_ref[slot] = jnp.where(keep, total, kept_ref[slot])

            @pl.when(slot >= 2)
            def _():
                sent_ref[slot - 2] = jnp.where(keep, total, sent_ref[slot - 2])


def flip(x, axis, bit):
    return lax.ppermute(x, axis, [(i, i ^ bit) for i in range(lax.axis_size(axis))])


def swap(x, axis, start):
    size = lax.axis_size(axis)
    pairs_of = [(i, i + 1) for i in range(start, size - 1, 2)]
    return lax.ppermute(x, axis, pairs_of + [(j, i) for i, j in pairs_of])


def behind(x, earlier):
    return lax.optimization_barrier((x, earlier))[0]


def exchange(kept, sent, prior):
    height, cols = prior.shape[0], prior.shape[1]
    even_row = lax.rem(lax.axis_index("rows"), 2) == 0
    even_col = lax.rem(lax.axis_index("cols"), 2) == 0
    first, last = prior[:, :HALO], prior[:, cols - HALO :]
    kept = kept + flip(sent, "rows", 1)
    side1 = swap(behind(jnp.where(even_col, first, last), kept), "cols", 1)
    kept = kept[0] + flip(kept[1], "rows", 2)
    side0 = swap(behind(jnp.where(even_col, last, first), kept), "cols", 0)
    hops = [("rows", 1 << b) for b in range(2, lax.axis_size("rows").bit_length() - 1)]
    hops += [("cols", 1 << b) for b in range(lax.axis_size("cols").bit_length() - 1)]
    stages = [kept]
    for axis, bit in hops:
        stages.append(stages[-1] + flip(stages[-1], axis, bit))
    left = jnp.where(even_col, side1, side0)
    right = jnp.where(even_col, side0, side1)

    def strip(lo, hi):
        return jnp.concatenate([prior[lo:hi], left[lo:hi], right[lo:hi]], 1)

    top, bottom = strip(0, HALO), strip(height - HALO, height)
    rows1 = swap(behind(jnp.where(even_row, top, bottom), stages[-3]), "rows", 1)
    rows0 = swap(behind(jnp.where(even_row, bottom, top), stages[-2]), "rows", 0)
    kept = stages[-1]
    other = flip(kept, "rows", 2)
    parts = kept, other, flip(kept, "rows", 1), flip(other, "rows", 1)
    return (side0, side1, rows0, rows1), parts


def update(x, taper, spread_w, gain_w):
    high, low_part = split(x)
    c_high, c_low = split(dot(jnp.concatenate([high, low_part, high], 1), spread_w) * taper)
    both = dot(c_high, gain_w)
    lanes = 2 * MEMBERS
    return x + (both[:, :lanes] + both[:, lanes:] + dot(c_low, gain_w[:, :lanes]))


def pair_up(a, b):
    low = low_lanes(a.shape)
    return jnp.where(low, a, swap_halves(b)), jnp.where(low, swap_halves(a), b)


def forecast_kernel(
    width, order, cells, mask, kern, mix, cell_ref, value_ref, var_ref, prior_ref,
    side0_ref, side1_ref, rows0_ref, rows1_ref, p0, p1, p2, p3,
    out_ref, field, predicted, table, place, spread0, gain0, spread1, gain1, lines,
):
    height, cols = prior_ref.shape[0], prior_ref.shape[1]
    my_row, my_col = lax.axis_index("rows"), lax.axis_index("cols")
    down, across = lax.axis_size("rows"), lax.axis_size("cols")
    mine = 2 * lax.rem(my_row, 2) + lax.rem(lax.div(my_row, 2), 2)
    for rel, part in enumerate((p0, p1, p2, p3)):
        predicted[jnp.bitwise_xor(rel, mine)] = part[...]
    pairs = height // 2
    depth = cols + 8
    lanes = 2 * MEMBERS
    even_row = lax.rem(my_row, 2) == 0
    even_col = lax.rem(my_col, 2) == 0

    def put(j, p, lo, a, b):
        first, second = pair_up(a, b)
        field[j, 2 * p, lo : lo + a.shape[0], :] = first
        field[j, 2 * p + 1, lo : lo + a.shape[0], :] = second

    for j in range(pairs + 3):
        for t in range(SPECIES):
            field[j, t, cols:depth, :] = jnp.zeros((8, lanes), F32)
    for p in range(SPECIES // 2):
        at = slice(128 * p, 128 * (p + 1))

        def left(r):
            return jnp.where(even_col, side1_ref[r, :, at], side0_ref[r, :, at])

        def right(r):
            return jnp.where(even_col, side0_ref[r, :, at], side1_ref[r, :, at])

        def above(r, lo, hi):
            return jnp.where(even_row, rows1_ref[r, lo:hi, at], rows0_ref[r, lo:hi, at])

        def below(r, lo, hi):
            return jnp.where(even_row, rows0_ref[r, lo:hi, at], rows1_ref[r, lo:hi, at])

        for j in range(pairs):
            put(j, p, 0, prior_ref[2 * j, :, at], prior_ref[2 * j + 1, :, at])
            put(j, p, cols, left(2 * j), left(2 * j + 1))
            put(j, p, cols + HALO, right(2 * j), right(2 * j + 1))
        for lo, hi in ((0, cols), (cols, cols + 2 * HALO)):
            put(pairs, p, lo, above(1, lo, hi), above(2, lo, hi))
            put(pairs + 1, p, lo, below(0, lo, hi), below(1, lo, hi))
            put(pairs + 2, p, lo, above(0, lo, hi), below(2, lo, hi))
    batches = [order[k] for k in range(BATCHES)]
    tiles = []
    for k in range(BATCHES):
        first = cells[batches[k], 0]
        tiles.append(lax.div(first, width * height) * across + lax.div(lax.rem(first, width), cols))
        table[k : k + 1, :] = cell_ref[pl.ds(batches[k], 1), :].astype(F32)
        table[8 + k : 9 + k, :] = value_ref[pl.ds(batches[k], 1), :]
        table[16 + k : 17 + k, :] = var_ref[pl.ds(batches[k], 1), :]
    cell_lane = table[0:8, :]
    row_lane = jnp.floor(cell_lane * (1.0 / width))
    col_lane = (cell_lane - row_lane * width) * (1.0 / HALFW)
    row_lane = row_lane * (1.0 / HALFW)
    row_col = jnp.transpose(row_lane)
    col_col = jnp.transpose(col_lane)
    value_col = jnp.transpose(table[8:16, :])
    var_col = jnp.transpose(table[16:24, :])
    low_obs = low_lanes((OBS, 2 * MEMBERS))
    index = lax.broadcasted_iota(jnp.int32, (depth, OBS), 0)
    to_left = (index >= cols) & (index < cols + HALO)
    to_right = index >= cols + HALO
    x_pos = jnp.where(to_left, index - cols - HALO, jnp.where(to_right, index - HALO, index))
    x_pos = (x_pos + my_col * cols).astype(F32) * (1.0 / HALFW)
    top_row = my_row * height
    zones = (
        jnp.maximum(my_row - 1, 0) * across, my_row * across, jnp.minimum(my_row + 1, down - 1) * across
    )
    sides = (jnp.maximum(my_col - 1, 0), my_col, jnp.minimum(my_col + 1, across - 1))
    row_pairs = [((top_row + 2 * j, 1), (top_row + 2 * j + 1, 1)) for j in range(pairs)]
    row_pairs += [
        ((top_row - 2, 0), (top_row - 1, 0)),
        ((top_row + height, 2), (top_row + height + 1, 2)),
        ((top_row - 3, 0), (top_row + height + 2, 2)),
    ]

    place[0:8, :] = row_lane
    place[8:16, :] = col_lane
    lane_index = lax.broadcasted_iota(jnp.int32, (OBS, BATCHES), 1)

    def column(values, k):
        return jnp.sum(jnp.where(lane_index == k, values, 0.0), axis=1, keepdims=True)

    def factors(k, spread_ref, gain_ref):
        block = predicted[lax.rem(k, 4)]
        turned_block = swap_halves(block)
        first_half = k < 4
        here = jnp.where(
            low_obs,
            jnp.where(first_half, block, turned_block),
            jnp.where(first_half, turned_block, block),
        )
        mean = jnp.sum(here, axis=1, keepdims=True) * (0.5 / MEMBERS)
        spread = here - mean
        variance = jnp.sum(spread * spread, axis=1, keepdims=True) * (0.5 / (MEMBERS - 1))
        var = column(var_col, k)
        denominator = variance + var
        shrink = 1.0 / (1.0 + jnp.sqrt(var / denominator))
        gain = ((column(value_col, k) - mean) - shrink * spread) / (denominator * (MEMBERS - 1))
        turned = jnp.transpose(spread)
        top = lax.broadcasted_iota(jnp.int32, turned.shape, 0) < MEMBERS
        zero = jnp.zeros_like(turned)
        wide = jnp.concatenate([jnp.where(top, turned, zero), jnp.where(top, zero, turned)], 1)
        wide_hi, wide_lo = split(wide)
        spread_ref[...] = jnp.concatenate([wide_hi, wide_hi, wide_lo], 0)
        tall = jnp.concatenate([jnp.where(low_obs, gain, zero), jnp.where(low_obs, zero, gain)], 0)
        gain_ref[...] = jnp.concatenate(split(tall), 1)

    def assimilate(k, spread_ref, gain_ref, next_spread_ref, next_gain_ref):
        batch = order[k]
        spread_w, gain_w = spread_ref[...], gain_ref[...]
        obs_row, obs_col = place[pl.ds(k, 1), :], place[pl.ds(8 + k, 1), :]
        for q in range(4):
            halves = []
            for later in (q, q + 4):
                dr = row_col[:, later : later + 1] - obs_row
                dc = col_col[:, later : later + 1] - obs_col
                on = (mask[batch, tiles[later]] > 0).astype(F32)
                halves.append(taper_weights(dr * dr + dc * dc) * on)
            predicted[q] = update(predicted[q], jnp.concatenate(halves, 1), spread_w, gain_w)
        factors(jnp.minimum(k + 1, BATCHES - 1), next_spread_ref, next_gain_ref)
        gap = x_pos - obs_col
        gap = gap * gap
        active = []
        for zone in zones:
            on = [(mask[batch, zone + side] > 0).astype(F32) for side in sides]
            active.append(jnp.where(to_left, on[0], jnp.where(to_right, on[2], on[1])))
        flat = (SPECIES * depth, lanes)
        for j in range(pairs + 3):
            halves = []
            for position, zone in row_pairs[j]:
                dy = position.astype(F32) * (1.0 / HALFW) - obs_row
                halves.append(taper_weights(gap + dy * dy) * active[zone])
            taper = jnp.concatenate([jnp.concatenate(halves, 1)] * SPECIES, 0)
            new = update(field[j].reshape(flat), taper, spread_w, gain_w)
            field[j] = new.reshape(SPECIES, depth, lanes)

    factors(jnp.int32(0), spread0, gain0)

    def two(i, carry):
        assimilate(2 * i, spread0, gain0, spread1, gain1)
        assimilate(2 * i + 1, spread1, gain1, spread0, gain0)
        return carry

    lax.fori_loop(0, BATCHES // 2, two, 0)

    sources = [pairs + 2, pairs] + list(range(pairs)) + [pairs + 1, pairs + 2]
    column = lax.broadcasted_iota(jnp.int32, (cols, 3 * depth), 1)
    third = column >= 2 * depth
    column = jnp.where(third, column - 2 * depth, jnp.where(column >= depth, column - depth, column))
    column = jnp.where(
        column < cols, column, jnp.where(column < cols + HALO, column - cols - HALO, column - HALO)
    )
    offset = column - lax.broadcasted_iota(jnp.int32, (cols, 3 * depth), 0) + HALO
    low = low_lanes((cols, lanes))

    def species(t, carry):
        bands = []
        for a in range(KW):
            band = jnp.zeros((cols, 3 * depth), F32)
            for e in range(KW):
                band = jnp.where(offset == e, kern[t, a * KW + e], band)
            high = band.astype(BF16).astype(F32)
            bands.append(jnp.where(third, band - high, high).astype(BF16))
        band = jnp.concatenate(bands, 0)
        for d in range(0, pairs + 4, 2):
            pieces = []
            for q in (d, d + 1):
                piece = field[sources[q], t]
                pieces.append(swap_halves(piece) if q in (0, pairs + 3) else piece)
            data = jnp.concatenate(pieces, 1)
            high = data.astype(BF16).astype(F32)
            data = jnp.concatenate([high, data - high, high], 0).astype(BF16)
            product = dot(band, data)
            lines[d] = product[:, :lanes]
            lines[d + 1] = product[:, lanes:]

        def part(q, a):
            return lines[q, a * cols : (a + 1) * cols, :]

        def odd(u):
            return swap_halves(part(u, 0) + part(u + 1, 2) + part(u + 2, 4) + part(u + 3, 6))

        before = odd(0)
        for j in range(pairs):
            after = odd(j + 1)
            straight = part(j + 1, 1) + part(j + 2, 3) + part(j + 3, 5)
            field[j, t, 0:cols, :] = straight + jnp.where(low, before, after)
            before = after
        return carry

    lax.fori_loop(0, SPECIES, species, 0)

    def mixed(j, carry):
        smooth = [field[j, t, 0:cols, :] for t in range(SPECIES)]
        for p in range(SPECIES // 2):
            total = []
            for s in (2 * p, 2 * p + 1):
                acc = mix[s, 0] * smooth[0]
                for t in range(1, SPECIES):
                    acc = acc + mix[s, t] * smooth[t]
                total.append(acc)
            out_ref[2 * j, :, 128 * p : 128 * (p + 1)] = jnp.where(low, total[0], swap_halves(total[1]))
            out_ref[2 * j + 1, :, 128 * p : 128 * (p + 1)] = jnp.where(
                low, swap_halves(total[0]), total[1]
            )
        return carry

    lax.fori_loop(0, pairs, mixed, 0)


def shards(prior, obs_cell, obs_weight, obs_value, obs_var, loc_mask, batch_order, kernel, mixing):
    height, cols, channels = prior.shape
    across = lax.axis_size("cols")
    width = cols * across
    pairs = height // 2
    lanes = 2 * MEMBERS
    kept, sent = pl.pallas_call(
        functools.partial(gather_kernel, width),
        out_shape=(jax.ShapeDtypeStruct((2, OBS, lanes), F32),) * 2,
        in_specs=[SMEM, SMEM, VMEM, VMEM],
        out_specs=(VMEM, VMEM),
        scratch_shapes=[pltpu.VMEM((OBS, channels), F32)],
        compiler_params=PARAMS,
        name="gather",
    )(batch_order, obs_cell, jnp.transpose(obs_weight, (0, 2, 1)), prior)
    halo, parts = exchange(kept, sent, prior)
    return pl.pallas_call(
        functools.partial(forecast_kernel, width),
        out_shape=jax.ShapeDtypeStruct((height, cols, channels), F32),
        in_specs=[SMEM] * 5 + [VMEM] * 12,
        out_specs=VMEM,
        scratch_shapes=[
            pltpu.VMEM((pairs + 3, SPECIES, cols + 8, lanes), F32),
            pltpu.VMEM((4, OBS, lanes), F32),
            pltpu.VMEM((24, OBS), F32),
            pltpu.VMEM((16, OBS), F32),
            pltpu.VMEM((3 * lanes, 2 * OBS), BF16),
            pltpu.VMEM((2 * OBS, 2 * lanes), BF16),
            pltpu.VMEM((3 * lanes, 2 * OBS), BF16),
            pltpu.VMEM((2 * OBS, 2 * lanes), BF16),
            pltpu.VMEM((pairs + 4, KW * cols, lanes), F32),
        ],
        compiler_params=PARAMS,
        name="forecast",
    )(
        batch_order, obs_cell, loc_mask, kernel.reshape(SPECIES, KW * KW), mixing,
        obs_cell, obs_value, obs_var, prior, *halo, *parts,
    )


def solution(mesh):
    return jax.shard_map(
        shards,
        mesh=mesh,
        in_specs=(P("rows", "cols", None), P(), P(), P(), P(), P(), P(), P(), P()),
        out_specs=P("rows", "cols", None),
        check_vma=False,
    )
```

```python
import functools

import jax
import jax.numpy as jnp
from jax import lax
from jax.experimental import pallas as pl
from jax.experimental.pallas import tpu as pltpu
from jax.sharding import PartitionSpec as P

BATCHES = 8
OBS = 128
SPECIES = 8
MEMBERS = 64
KW = 7
HALO = KW // 2
HALFW = 48
BF16 = jnp.bfloat16
F32 = jnp.float32
VMEM = pl.BlockSpec(memory_space=pltpu.VMEM)
SMEM = pl.BlockSpec(memory_space=pltpu.SMEM)
PARAMS = pltpu.CompilerParams(vmem_limit_bytes=56 << 20)


def split(x):
    high = x.astype(BF16)
    return high, (x - high.astype(F32)).astype(BF16)


def dot(a, b):
    return jnp.dot(a, b, preferred_element_type=F32)


def swap_halves(x):
    return pltpu.roll(x, MEMBERS, axis=x.ndim - 1)


def low_lanes(shape):
    return lax.broadcasted_iota(jnp.int32, shape, len(shape) - 1) < MEMBERS


def taper_weights(squared):
    inverse = lax.rsqrt(jnp.maximum(squared, 1e-4))
    ratio = squared * inverse
    inner = 1.0 - (ratio * ratio) * (5.0 / 3.0 - ratio * (0.625 + ratio * (0.5 - 0.25 * ratio)))
    left = jnp.maximum(2.0 - ratio, 0.0)
    left = left * left
    outer = (left * left) * (((ratio + 2.0) * ratio - 0.5) * (inverse * (1.0 / 12.0)))
    return jnp.where(ratio <= 1.0, inner, outer)


def gather_kernel(width, order, cells, weight_ref, prior_ref, kept_ref, sent_ref, picked):
    height, cols = prior_ref.shape[0], prior_ref.shape[1]
    my_row, my_col = lax.axis_index("rows"), lax.axis_index("cols")
    mine = 2 * lax.rem(my_row, 2) + lax.rem(lax.div(my_row, 2), 2)
    corner = my_row * height * width + my_col * cols
    kept_ref[...] = jnp.zeros_like(kept_ref)
    sent_ref[...] = jnp.zeros_like(sent_ref)
    for k in range(BATCHES):
        batch = order[k]
        first = cells[batch, 0]
        owner = (lax.div(first, width * height) == my_row) & (
            lax.div(lax.rem(first, width), cols) == my_col
        )

        @pl.when(owner)
        def _():
            def one(i, carry):
                cell = cells[batch, i] - corner
                row = lax.div(cell, width)
                picked[pl.ds(i, 1), :] = prior_ref[row, pl.ds(cell - row * width, 1), :]
                return carry

            lax.fori_loop(0, OBS, one, 0, unroll=8)
            weights = jnp.transpose(weight_ref[batch])
            low = low_lanes((OBS, 2 * MEMBERS))
            total = jnp.zeros((OBS, 2 * MEMBERS), F32)
            for p in range(SPECIES // 2):
                scale = jnp.where(low, weights[:, 2 * p : 2 * p + 1], weights[:, 2 * p + 1 : 2 * p + 2])
                total = total + scale * picked[:, 128 * p : 128 * (p + 1)]
            total = total + swap_halves(total)
            slot = jnp.bitwise_xor(k % 4, mine)
            keep = low if k < 4 else jnp.logical_not(low)

            @pl.when(slot < 2)
            def _():
                kept_ref[slot] = jnp.where(keep, total, kept_ref[slot])

            @pl.when(slot >= 2)
            def _():
                sent_ref[slot - 2] = jnp.where(keep, total, sent_ref[slot - 2])


def flip(x, axis, bit):
    return lax.ppermute(x, axis, [(i, i ^ bit) for i in range(lax.axis_size(axis))])


def swap(x, axis, start):
    size = lax.axis_size(axis)
    pairs_of = [(i, i + 1) for i in range(start, size - 1, 2)]
    return lax.ppermute(x, axis, pairs_of + [(j, i) for i, j in pairs_of])


def behind(x, earlier):
    return lax.optimization_barrier((x, earlier))[0]


def exchange(kept, sent, prior):
    height, cols = prior.shape[0], prior.shape[1]
    even_row = lax.rem(lax.axis_index("rows"), 2) == 0
    even_col = lax.rem(lax.axis_index("cols"), 2) == 0
    first, last = prior[:, :HALO], prior[:, cols - HALO :]
    kept = kept + flip(sent, "rows", 1)
    side1 = swap(behind(jnp.where(even_col, first, last), kept), "cols", 1)
    kept = kept[0] + flip(kept[1], "rows", 2)
    side0 = swap(behind(jnp.where(even_col, last, first), kept), "cols", 0)
    hops = [("rows", 1 << b) for b in range(2, lax.axis_size("rows").bit_length() - 1)]
    hops += [("cols", 1 << b) for b in range(lax.axis_size("cols").bit_length() - 1)]
    stages = [kept]
    for axis, bit in hops:
        stages.append(stages[-1] + flip(stages[-1], axis, bit))
    left = jnp.where(even_col, side1, side0)
    right = jnp.where(even_col, side0, side1)

    def strip(lo, hi):
        return jnp.concatenate([prior[lo:hi], left[lo:hi], right[lo:hi]], 1)

    top, bottom = strip(0, HALO), strip(height - HALO, height)
    rows1 = swap(behind(jnp.where(even_row, top, bottom), stages[-3]), "rows", 1)
    rows0 = swap(behind(jnp.where(even_row, bottom, top), stages[-2]), "rows", 0)
    kept = stages[-1]
    other = flip(kept, "rows", 2)
    parts = kept, other, flip(kept, "rows", 1), flip(other, "rows", 1)
    return (side0, side1, rows0, rows1), parts


def update(x, taper, spread_w, gain_w):
    high, low_part = split(x)
    c_high, c_low = split(dot(jnp.concatenate([high, low_part, high], 1), spread_w) * taper)
    both = dot(c_high, gain_w)
    lanes = 2 * MEMBERS
    return x + (both[:, :lanes] + both[:, lanes:] + dot(c_low, gain_w[:, :lanes]))


def pair_up(a, b):
    low = low_lanes(a.shape)
    return jnp.where(low, a, swap_halves(b)), jnp.where(low, swap_halves(a), b)


def forecast_kernel(
    width, order, cells, mask, kern, mix, cell_ref, value_ref, var_ref, prior_ref,
    side0_ref, side1_ref, rows0_ref, rows1_ref, p0, p1, p2, p3,
    out_ref, field, predicted, table, place, spread0, gain0, spread1, gain1, lines,
):
    height, cols = prior_ref.shape[0], prior_ref.shape[1]
    my_row, my_col = lax.axis_index("rows"), lax.axis_index("cols")
    down, across = lax.axis_size("rows"), lax.axis_size("cols")
    mine = 2 * lax.rem(my_row, 2) + lax.rem(lax.div(my_row, 2), 2)
    for rel, part in enumerate((p0, p1, p2, p3)):
        predicted[jnp.bitwise_xor(rel, mine)] = part[...]
    pairs = height // 2
    depth = cols + 8
    lanes = 2 * MEMBERS
    even_row = lax.rem(my_row, 2) == 0
    even_col = lax.rem(my_col, 2) == 0

    def put(j, p, lo, a, b):
        first, second = pair_up(a, b)
        field[j, 2 * p, lo : lo + a.shape[0], :] = first
        field[j, 2 * p + 1, lo : lo + a.shape[0], :] = second

    for j in range(pairs + 3):
        for t in range(SPECIES):
            field[j, t, cols:depth, :] = jnp.zeros((8, lanes), F32)
    for p in range(SPECIES // 2):
        at = slice(128 * p, 128 * (p + 1))

        def left(r):
            return jnp.where(even_col, side1_ref[r, :, at], side0_ref[r, :, at])

        def right(r):
            return jnp.where(even_col, side0_ref[r, :, at], side1_ref[r, :, at])

        def above(r, lo, hi):
            return jnp.where(even_row, rows1_ref[r, lo:hi, at], rows0_ref[r, lo:hi, at])

        def below(r, lo, hi):
            return jnp.where(even_row, rows0_ref[r, lo:hi, at], rows1_ref[r, lo:hi, at])

        for j in range(pairs):
            put(j, p, 0, prior_ref[2 * j, :, at], prior_ref[2 * j + 1, :, at])
            put(j, p, cols, left(2 * j), left(2 * j + 1))
            put(j, p, cols + HALO, right(2 * j), right(2 * j + 1))
        for lo, hi in ((0, cols), (cols, cols + 2 * HALO)):
            put(pairs, p, lo, above(1, lo, hi), above(2, lo, hi))
            put(pairs + 1, p, lo, below(0, lo, hi), below(1, lo, hi))
            put(pairs + 2, p, lo, above(0, lo, hi), below(2, lo, hi))
    batches = [order[k] for k in range(BATCHES)]
    tiles = []
    for k in range(BATCHES):
        first = cells[batches[k], 0]
        tiles.append(lax.div(first, width * height) * across + lax.div(lax.rem(first, width), cols))
        table[k : k + 1, :] = cell_ref[pl.ds(batches[k], 1), :].astype(F32)
        table[8 + k : 9 + k, :] = value_ref[pl.ds(batches[k], 1), :]
        table[16 + k : 17 + k, :] = var_ref[pl.ds(batches[k], 1), :]
    cell_lane = table[0:8, :]
    row_lane = jnp.floor(cell_lane * (1.0 / width))
    col_lane = (cell_lane - row_lane * width) * (1.0 / HALFW)
    row_lane = row_lane * (1.0 / HALFW)
    row_col = jnp.transpose(row_lane)
    col_col = jnp.transpose(col_lane)
    value_col = jnp.transpose(table[8:16, :])
    var_col = jnp.transpose(table[16:24, :])
    low_obs = low_lanes((OBS, 2 * MEMBERS))
    index = lax.broadcasted_iota(jnp.int32, (depth, OBS), 0)
    to_left = (index >= cols) & (index < cols + HALO)
    to_right = index >= cols + HALO
    x_pos = jnp.where(to_left, index - cols - HALO, jnp.where(to_right, index - HALO, index))
    x_pos = (x_pos + my_col * cols).astype(F32) * (1.0 / HALFW)
    top_row = my_row * height
    zones = (
        jnp.maximum(my_row - 1, 0) * across, my_row * across, jnp.minimum(my_row + 1, down - 1) * across
    )
    sides = (jnp.maximum(my_col - 1, 0), my_col, jnp.minimum(my_col + 1, across - 1))
    row_pairs = [((top_row + 2 * j, 1), (top_row + 2 * j + 1, 1)) for j in range(pairs)]
    row_pairs += [
        ((top_row - 2, 0), (top_row - 1, 0)),
        ((top_row + height, 2), (top_row + height + 1, 2)),
        ((top_row - 3, 0), (top_row + height + 2, 2)),
    ]

    place[0:8, :] = row_lane
    place[8:16, :] = col_lane
    lane_index = lax.broadcasted_iota(jnp.int32, (OBS, BATCHES), 1)

    def column(values, k):
        return jnp.sum(jnp.where(lane_index == k, values, 0.0), axis=1, keepdims=True)

    def factors(k, spread_ref, gain_ref):
        block = predicted[lax.rem(k, 4)]
        turned_block = swap_halves(block)
        first_half = k < 4
        here = jnp.where(
            low_obs,
            jnp.where(first_half, block, turned_block),
            jnp.where(first_half, turned_block, block),
        )
        mean = jnp.sum(here, axis=1, keepdims=True) * (0.5 / MEMBERS)
        spread = here - mean
        variance = jnp.sum(spread * spread, axis=1, keepdims=True) * (0.5 / (MEMBERS - 1))
        var = column(var_col, k)
        denominator = variance + var
        shrink = 1.0 / (1.0 + jnp.sqrt(var / denominator))
        gain = ((column(value_col, k) - mean) - shrink * spread) / (denominator * (MEMBERS - 1))
        turned = jnp.transpose(spread)
        top = lax.broadcasted_iota(jnp.int32, turned.shape, 0) < MEMBERS
        zero = jnp.zeros_like(turned)
        wide = jnp.concatenate([jnp.where(top, turned, zero), jnp.where(top, zero, turned)], 1)
        wide_hi, wide_lo = split(wide)
        spread_ref[...] = jnp.concatenate([wide_hi, wide_hi, wide_lo], 0)
        tall = jnp.concatenate([jnp.where(low_obs, gain, zero), jnp.where(low_obs, zero, gain)], 0)
        gain_ref[...] = jnp.concatenate(split(tall), 1)

    def assimilate(k, waiting, spread_ref, gain_ref, next_spread_ref, next_gain_ref):
        batch = order[k]
        spread_w, gain_w = spread_ref[...], gain_ref[...]
        obs_row, obs_col = place[pl.ds(k, 1), :], place[pl.ds(8 + k, 1), :]
        for q in waiting:
            halves = []
            for later in (q, q + 4):
                dr = row_col[:, later : later + 1] - obs_row
                dc = col_col[:, later : later + 1] - obs_col
                on = (mask[batch, tiles[later]] > 0).astype(F32)
                halves.append(taper_weights(dr * dr + dc * dc) * on)
            predicted[q] = update(predicted[q], jnp.concatenate(halves, 1), spread_w, gain_w)
        factors(jnp.minimum(k + 1, BATCHES - 1), next_spread_ref, next_gain_ref)
        gap = x_pos - obs_col
        gap = gap * gap
        active = []
        for zone in zones:
            on = [(mask[batch, zone + side] > 0).astype(F32) for side in sides]
            active.append(jnp.where(to_left, on[0], jnp.where(to_right, on[2], on[1])))
        flat = (SPECIES * depth, lanes)
        for j in range(pairs + 3):
            halves = []
            for position, zone in row_pairs[j]:
                dy = position.astype(F32) * (1.0 / HALFW) - obs_row
                halves.append(taper_weights(gap + dy * dy) * active[zone])
            taper = jnp.concatenate([jnp.concatenate(halves, 1)] * SPECIES, 0)
            new = update(field[j].reshape(flat), taper, spread_w, gain_w)
            field[j] = new.reshape(SPECIES, depth, lanes)

    factors(jnp.int32(0), spread0, gain0)

    def two(i, carry):
        assimilate(2 * i, (0, 1, 2, 3), spread0, gain0, spread1, gain1)
        assimilate(2 * i + 1, (0, 1, 2, 3), spread1, gain1, spread0, gain0)
        return carry

    def last_two(i, carry):
        assimilate(2 * i, (1, 2, 3), spread0, gain0, spread1, gain1)
        assimilate(2 * i + 1, (2, 3), spread1, gain1, spread0, gain0)
        return carry

    lax.fori_loop(0, 2, two, 0)
    lax.fori_loop(2, 4, last_two, 0)

    sources = [pairs + 2, pairs] + list(range(pairs)) + [pairs + 1, pairs + 2]
    column = lax.broadcasted_iota(jnp.int32, (cols, 3 * depth), 1)
    third = column >= 2 * depth
    column = jnp.where(third, column - 2 * depth, jnp.where(column >= depth, column - depth, column))
    column = jnp.where(
        column < cols, column, jnp.where(column < cols + HALO, column - cols - HALO, column - HALO)
    )
    offset = column - lax.broadcasted_iota(jnp.int32, (cols, 3 * depth), 0) + HALO
    low = low_lanes((cols, lanes))

    def species(t, carry):
        bands = []
        for a in range(KW):
            band = jnp.zeros((cols, 3 * depth), F32)
            for e in range(KW):
                band = jnp.where(offset == e, kern[a, t, e], band)
            high = band.astype(BF16).astype(F32)
            bands.append(jnp.where(third, band - high, high).astype(BF16))
        band = jnp.concatenate(bands, 0)
        for d in range(0, pairs + 4, 2):
            pieces = []
            for q in (d, d + 1):
                piece = field[sources[q], t]
                pieces.append(swap_halves(piece) if q in (0, pairs + 3) else piece)
            data = jnp.concatenate(pieces, 1)
            high = data.astype(BF16).astype(F32)
            data = jnp.concatenate([high, data - high, high], 0).astype(BF16)
            product = dot(band, data)
            lines[d] = product[:, :lanes]
            lines[d + 1] = product[:, lanes:]

        def part(q, a):
            return lines[q, a * cols : (a + 1) * cols, :]

        def odd(u):
            return swap_halves(part(u, 0) + part(u + 1, 2) + part(u + 2, 4) + part(u + 3, 6))

        before = odd(0)
        for j in range(pairs):
            after = odd(j + 1)
            straight = part(j + 1, 1) + part(j + 2, 3) + part(j + 3, 5)
            field[j, t, 0:cols, :] = straight + jnp.where(low, before, after)
            before = after
        return carry

    lax.fori_loop(0, SPECIES, species, 0, unroll=4)

    def mixed(j, carry):
        smooth = [field[j, t, 0:cols, :] for t in range(SPECIES)]
        for p in range(SPECIES // 2):
            total = []
            for s in (2 * p, 2 * p + 1):
                acc = mix[s, 0] * smooth[0]
                for t in range(1, SPECIES):
                    acc = acc + mix[s, t] * smooth[t]
                total.append(acc)
            out_ref[2 * j, :, 128 * p : 128 * (p + 1)] = jnp.where(low, total[0], swap_halves(total[1]))
            out_ref[2 * j + 1, :, 128 * p : 128 * (p + 1)] = jnp.where(
                low, swap_halves(total[0]), total[1]
            )
        return carry

    lax.fori_loop(0, pairs, mixed, 0, unroll=2)


def shards(prior, obs_cell, obs_weight, obs_value, obs_var, loc_mask, batch_order, kernel, mixing):
    height, cols, channels = prior.shape
    across = lax.axis_size("cols")
    width = cols * across
    pairs = height // 2
    lanes = 2 * MEMBERS
    kept, sent = pl.pallas_call(
        functools.partial(gather_kernel, width),
        out_shape=(jax.ShapeDtypeStruct((2, OBS, lanes), F32),) * 2,
        in_specs=[SMEM, SMEM, VMEM, VMEM],
        out_specs=(VMEM, VMEM),
        scratch_shapes=[pltpu.VMEM((OBS, channels), F32)],
        compiler_params=PARAMS,
        name="gather",
    )(batch_order, obs_cell, jnp.transpose(obs_weight, (0, 2, 1)), prior)
    halo, parts = exchange(kept, sent, prior)
    return pl.pallas_call(
        functools.partial(forecast_kernel, width),
        out_shape=jax.ShapeDtypeStruct((height, cols, channels), F32),
        in_specs=[SMEM] * 5 + [VMEM] * 12,
        out_specs=VMEM,
        scratch_shapes=[
            pltpu.VMEM((pairs + 3, SPECIES, cols + 8, lanes), F32),
            pltpu.VMEM((4, OBS, lanes), F32),
            pltpu.VMEM((24, OBS), F32),
            pltpu.VMEM((16, OBS), F32),
            pltpu.VMEM((3 * lanes, 2 * OBS), BF16),
            pltpu.VMEM((2 * OBS, 2 * lanes), BF16),
            pltpu.VMEM((3 * lanes, 2 * OBS), BF16),
            pltpu.VMEM((2 * OBS, 2 * lanes), BF16),
            pltpu.VMEM((pairs + 4, KW * cols, lanes), F32),
        ],
        compiler_params=PARAMS,
        name="forecast",
    )(
        batch_order, obs_cell, loc_mask, jnp.transpose(kernel, (1, 0, 2)), mixing,
        obs_cell, obs_value, obs_var, prior, *halo, *parts,
    )


def solution(mesh):
    return jax.shard_map(
        shards,
        mesh=mesh,
        in_specs=(P("rows", "cols", None), P(), P(), P(), P(), P(), P(), P(), P()),
        out_specs=P("rows", "cols", None),
        check_vma=False,
    )
```

```python
import functools

import jax
import jax.numpy as jnp
from jax import lax
from jax.experimental import pallas as pl
from jax.experimental.pallas import tpu as pltpu
from jax.sharding import PartitionSpec as P

BATCHES = 8
OBS = 128
SPECIES = 8
MEMBERS = 64
KW = 7
HALO = KW // 2
HALFW = 48
BF16 = jnp.bfloat16
F32 = jnp.float32
VMEM = pl.BlockSpec(memory_space=pltpu.VMEM)
SMEM = pl.BlockSpec(memory_space=pltpu.SMEM)
PARAMS = pltpu.CompilerParams(vmem_limit_bytes=56 << 20)


def split(x):
    high = x.astype(BF16)
    return high, (x - high.astype(F32)).astype(BF16)


def dot(a, b):
    return jnp.dot(a, b, preferred_element_type=F32)


def swap_halves(x):
    return pltpu.roll(x, MEMBERS, axis=x.ndim - 1)


def low_lanes(shape):
    return lax.broadcasted_iota(jnp.int32, shape, len(shape) - 1) < MEMBERS


def taper_weights(squared):
    inverse = lax.rsqrt(jnp.maximum(squared, 1e-4))
    ratio = squared * inverse
    inner = 1.0 - (ratio * ratio) * (5.0 / 3.0 - ratio * (0.625 + ratio * (0.5 - 0.25 * ratio)))
    left = jnp.maximum(2.0 - ratio, 0.0)
    left = left * left
    outer = (left * left) * (((ratio + 2.0) * ratio - 0.5) * (inverse * (1.0 / 12.0)))
    return jnp.where(ratio <= 1.0, inner, outer)


def gather_kernel(width, order, cells, weight_ref, prior_ref, kept_ref, sent_ref, picked):
    height, cols = prior_ref.shape[0], prior_ref.shape[1]
    my_row, my_col = lax.axis_index("rows"), lax.axis_index("cols")
    mine = 2 * lax.rem(my_row, 2) + lax.rem(lax.div(my_row, 2), 2)
    corner = my_row * height * width + my_col * cols
    kept_ref[...] = jnp.zeros_like(kept_ref)
    sent_ref[...] = jnp.zeros_like(sent_ref)
    for k in range(BATCHES):
        batch = order[k]
        first = cells[batch, 0]
        owner = (lax.div(first, width * height) == my_row) & (
            lax.div(lax.rem(first, width), cols) == my_col
        )

        @pl.when(owner)
        def _():
            def one(i, carry):
                cell = cells[batch, i] - corner
                row = lax.div(cell, width)
                picked[pl.ds(i, 1), :] = prior_ref[row, pl.ds(cell - row * width, 1), :]
                return carry

            lax.fori_loop(0, OBS, one, 0, unroll=8)
            weights = jnp.transpose(weight_ref[batch])
            low = low_lanes((OBS, 2 * MEMBERS))
            total = jnp.zeros((OBS, 2 * MEMBERS), F32)
            for p in range(SPECIES // 2):
                scale = jnp.where(low, weights[:, 2 * p : 2 * p + 1], weights[:, 2 * p + 1 : 2 * p + 2])
                total = total + scale * picked[:, 128 * p : 128 * (p + 1)]
            total = total + swap_halves(total)
            slot = jnp.bitwise_xor(k % 4, mine)
            keep = low if k < 4 else jnp.logical_not(low)

            @pl.when(slot < 2)
            def _():
                kept_ref[slot] = jnp.where(keep, total, kept_ref[slot])

            @pl.when(slot >= 2)
            def _():
                sent_ref[slot - 2] = jnp.where(keep, total, sent_ref[slot - 2])


def flip(x, axis, bit):
    return lax.ppermute(x, axis, [(i, i ^ bit) for i in range(lax.axis_size(axis))])


def swap(x, axis, start):
    size = lax.axis_size(axis)
    pairs_of = [(i, i + 1) for i in range(start, size - 1, 2)]
    return lax.ppermute(x, axis, pairs_of + [(j, i) for i, j in pairs_of])


def behind(x, earlier):
    return lax.optimization_barrier((x, earlier))[0]


def exchange(kept, sent, prior):
    height, cols = prior.shape[0], prior.shape[1]
    even_row = lax.rem(lax.axis_index("rows"), 2) == 0
    even_col = lax.rem(lax.axis_index("cols"), 2) == 0
    first, last = prior[:, :HALO], prior[:, cols - HALO :]
    kept = kept + flip(sent, "rows", 1)
    side1 = swap(behind(jnp.where(even_col, first, last), kept), "cols", 1)
    kept = kept[0] + flip(kept[1], "rows", 2)
    side0 = swap(behind(jnp.where(even_col, last, first), kept), "cols", 0)
    hops = [("rows", 1 << b) for b in range(2, lax.axis_size("rows").bit_length() - 1)]
    hops += [("cols", 1 << b) for b in range(lax.axis_size("cols").bit_length() - 1)]
    stages = [kept]
    for axis, bit in hops:
        stages.append(stages[-1] + flip(stages[-1], axis, bit))
    left = jnp.where(even_col, side1, side0)
    right = jnp.where(even_col, side0, side1)

    def strip(lo, hi):
        return jnp.concatenate([prior[lo:hi], left[lo:hi], right[lo:hi]], 1)

    top, bottom = strip(0, HALO), strip(height - HALO, height)
    rows1 = swap(behind(jnp.where(even_row, top, bottom), stages[-3]), "rows", 1)
    rows0 = swap(behind(jnp.where(even_row, bottom, top), stages[-2]), "rows", 0)
    kept = stages[-1]
    other = flip(kept, "rows", 2)
    parts = kept, other, flip(kept, "rows", 1), flip(other, "rows", 1)
    return (side0, side1, rows0, rows1), parts


def update(x, taper, spread_w, gain_w):
    high, low_part = split(x)
    c_high, c_low = split(dot(jnp.concatenate([high, low_part, high], 1), spread_w) * taper)
    both = dot(jnp.concatenate([c_high, c_low], 1), gain_w)
    lanes = 2 * MEMBERS
    return x + (both[:, :lanes] + both[:, lanes:])


def pair_up(a, b):
    low = low_lanes(a.shape)
    return jnp.where(low, a, swap_halves(b)), jnp.where(low, swap_halves(a), b)


def forecast_kernel(
    width, order, cells, mask, kern, mix, cell_ref, value_ref, var_ref, source_ref,
    side0_ref, side1_ref, rows0_ref, rows1_ref, p0, p1, p2, p3,
    out_ref, field, predicted, table, place, spread0, gain0, spread1, gain1, lines,
    prior_ref, ready, came, done,
):
    arrive = pltpu.make_async_copy(source_ref, prior_ref, came)
    arrive.start()
    height, cols = prior_ref.shape[0], prior_ref.shape[1]
    my_row, my_col = lax.axis_index("rows"), lax.axis_index("cols")
    down, across = lax.axis_size("rows"), lax.axis_size("cols")
    mine = 2 * lax.rem(my_row, 2) + lax.rem(lax.div(my_row, 2), 2)
    for rel, part in enumerate((p0, p1, p2, p3)):
        predicted[jnp.bitwise_xor(rel, mine)] = part[...]
    pairs = height // 2
    depth = cols + 8
    lanes = 2 * MEMBERS
    even_row = lax.rem(my_row, 2) == 0
    even_col = lax.rem(my_col, 2) == 0

    batches = [order[k] for k in range(BATCHES)]
    tiles = []
    for k in range(BATCHES):
        first = cells[batches[k], 0]
        tiles.append(lax.div(first, width * height) * across + lax.div(lax.rem(first, width), cols))
        table[k : k + 1, :] = cell_ref[pl.ds(batches[k], 1), :].astype(F32)
        table[8 + k : 9 + k, :] = value_ref[pl.ds(batches[k], 1), :]
        table[16 + k : 17 + k, :] = var_ref[pl.ds(batches[k], 1), :]
    cell_lane = table[0:8, :]
    row_lane = jnp.floor(cell_lane * (1.0 / width))
    col_lane = (cell_lane - row_lane * width) * (1.0 / HALFW)
    row_lane = row_lane * (1.0 / HALFW)
    row_col = jnp.transpose(row_lane)
    col_col = jnp.transpose(col_lane)
    value_col = jnp.transpose(table[8:16, :])
    var_col = jnp.transpose(table[16:24, :])
    low_obs = low_lanes((OBS, 2 * MEMBERS))
    index = lax.broadcasted_iota(jnp.int32, (depth, OBS), 0)
    to_left = (index >= cols) & (index < cols + HALO)
    to_right = index >= cols + HALO
    x_pos = jnp.where(to_left, index - cols - HALO, jnp.where(to_right, index - HALO, index))
    x_pos = (x_pos + my_col * cols).astype(F32) * (1.0 / HALFW)
    top_row = my_row * height
    zones = (
        jnp.maximum(my_row - 1, 0) * across, my_row * across, jnp.minimum(my_row + 1, down - 1) * across
    )
    sides = (jnp.maximum(my_col - 1, 0), my_col, jnp.minimum(my_col + 1, across - 1))
    row_pairs = [((top_row + 2 * j, 1), (top_row + 2 * j + 1, 1)) for j in range(pairs)]
    row_pairs += [
        ((top_row - 2, 0), (top_row - 1, 0)),
        ((top_row + height, 2), (top_row + height + 1, 2)),
        ((top_row - 3, 0), (top_row + height + 2, 2)),
    ]

    place[0:8, :] = row_lane
    place[8:16, :] = col_lane
    lane_index = lax.broadcasted_iota(jnp.int32, (OBS, BATCHES), 1)

    def column(values, k):
        return jnp.sum(jnp.where(lane_index == k, values, 0.0), axis=1, keepdims=True)

    def factors(k, spread_ref, gain_ref):
        block = predicted[lax.rem(k, 4)]
        turned_block = swap_halves(block)
        first_half = k < 4
        here = jnp.where(
            low_obs,
            jnp.where(first_half, block, turned_block),
            jnp.where(first_half, turned_block, block),
        )
        mean = jnp.sum(here, axis=1, keepdims=True) * (0.5 / MEMBERS)
        spread = here - mean
        variance = jnp.sum(spread * spread, axis=1, keepdims=True) * (0.5 / (MEMBERS - 1))
        var = column(var_col, k)
        denominator = variance + var
        shrink = 1.0 / (1.0 + jnp.sqrt(var / denominator))
        gain = ((column(value_col, k) - mean) - shrink * spread) / (denominator * (MEMBERS - 1))
        turned = jnp.transpose(spread)
        top = lax.broadcasted_iota(jnp.int32, turned.shape, 0) < MEMBERS
        zero = jnp.zeros_like(turned)
        wide = jnp.concatenate([jnp.where(top, turned, zero), jnp.where(top, zero, turned)], 1)
        wide_hi, wide_lo = split(wide)
        spread_ref[...] = jnp.concatenate([wide_hi, wide_hi, wide_lo], 0)
        tall = jnp.concatenate([jnp.where(low_obs, gain, zero), jnp.where(low_obs, zero, gain)], 0)
        tall_hi, tall_lo = split(tall)
        gain_ref[...] = jnp.concatenate([jnp.concatenate([tall_hi, tall_lo], 1), jnp.concatenate([tall_hi, jnp.zeros_like(tall_lo)], 1)], 0)

    def assimilate(k, waiting, spread_ref, gain_ref, next_spread_ref, next_gain_ref):
        batch = order[k]
        spread_w, gain_w = spread_ref[...], gain_ref[...]
        obs_row, obs_col = place[pl.ds(k, 1), :], place[pl.ds(8 + k, 1), :]
        for q in waiting:
            halves = []
            for later in (q, q + 4):
                dr = row_col[:, later : later + 1] - obs_row
                dc = col_col[:, later : later + 1] - obs_col
                on = (mask[batch, tiles[later]] > 0).astype(F32)
                halves.append(taper_weights(dr * dr + dc * dc) * on)
            predicted[q] = update(predicted[q], jnp.concatenate(halves, 1), spread_w, gain_w)
        if next_spread_ref is not None:
            factors(k + 1, next_spread_ref, next_gain_ref)
        gap = x_pos - obs_col
        gap = gap * gap
        active = []
        for zone in zones:
            on = [(mask[batch, zone + side] > 0).astype(F32) for side in sides]
            active.append(jnp.where(to_left, on[0], jnp.where(to_right, on[2], on[1])))
        flat = (SPECIES * depth, lanes)
        for j in range(pairs + 3):
            halves = []
            for position, zone in row_pairs[j]:
                dy = position.astype(F32) * (1.0 / HALFW) - obs_row
                halves.append(taper_weights(gap + dy * dy) * active[zone])
            taper = jnp.concatenate([jnp.concatenate(halves, 1)] * SPECIES, 0)
            new = update(field[j].reshape(flat), taper, spread_w, gain_w)
            field[j] = new.reshape(SPECIES, depth, lanes)

    factors(jnp.int32(0), spread0, gain0)
    arrive.wait()

    def put(j, p, lo, a, b):
        first, second = pair_up(a, b)
        field[j, 2 * p, lo : lo + a.shape[0], :] = first
        field[j, 2 * p + 1, lo : lo + a.shape[0], :] = second

    for j in range(pairs + 3):
        for t in range(SPECIES):
            field[j, t, cols:depth, :] = jnp.zeros((8, lanes), F32)
    for p in range(SPECIES // 2):
        at = slice(128 * p, 128 * (p + 1))

        def left(r):
            return jnp.where(even_col, side1_ref[r, :, at], side0_ref[r, :, at])

        def right(r):
            return jnp.where(even_col, side0_ref[r, :, at], side1_ref[r, :, at])

        def above(r, lo, hi):
            return jnp.where(even_row, rows1_ref[r, lo:hi, at], rows0_ref[r, lo:hi, at])

        def below(r, lo, hi):
            return jnp.where(even_row, rows0_ref[r, lo:hi, at], rows1_ref[r, lo:hi, at])

        for j in range(pairs):
            put(j, p, 0, prior_ref[2 * j, :, at], prior_ref[2 * j + 1, :, at])
            put(j, p, cols, left(2 * j), left(2 * j + 1))
            put(j, p, cols + HALO, right(2 * j), right(2 * j + 1))
        for lo, hi in ((0, cols), (cols, cols + 2 * HALO)):
            put(pairs, p, lo, above(1, lo, hi), above(2, lo, hi))
            put(pairs + 1, p, lo, below(0, lo, hi), below(1, lo, hi))
            put(pairs + 2, p, lo, above(0, lo, hi), below(2, lo, hi))


    def two(i, carry):
        assimilate(2 * i, (0, 1, 2, 3), spread0, gain0, spread1, gain1)
        assimilate(2 * i + 1, (0, 1, 2, 3), spread1, gain1, spread0, gain0)
        return carry

    lax.fori_loop(0, 2, two, 0)
    assimilate(4, (1, 2, 3), spread0, gain0, spread1, gain1)
    assimilate(5, (2, 3), spread1, gain1, spread0, gain0)
    assimilate(6, (3,), spread0, gain0, spread1, gain1)
    assimilate(7, (), spread1, gain1, None, None)

    sources = [pairs + 2, pairs] + list(range(pairs)) + [pairs + 1, pairs + 2]
    column = lax.broadcasted_iota(jnp.int32, (cols, 3 * depth), 1)
    third = column >= 2 * depth
    column = jnp.where(third, column - 2 * depth, jnp.where(column >= depth, column - depth, column))
    column = jnp.where(
        column < cols, column, jnp.where(column < cols + HALO, column - cols - HALO, column - HALO)
    )
    offset = column - lax.broadcasted_iota(jnp.int32, (cols, 3 * depth), 0) + HALO
    low = low_lanes((cols, lanes))

    def species(t, carry):
        bands = []
        for a in range(KW):
            band = jnp.zeros((cols, 3 * depth), F32)
            for e in range(KW):
                band = jnp.where(offset == e, kern[a, t, e], band)
            high = band.astype(BF16).astype(F32)
            bands.append(jnp.where(third, band - high, high).astype(BF16))
        band = jnp.concatenate(bands, 0)
        for d in range(0, pairs + 4, 2):
            pieces = []
            for q in (d, d + 1):
                piece = field[sources[q], t]
                pieces.append(swap_halves(piece) if q in (0, pairs + 3) else piece)
            data = jnp.concatenate(pieces, 1)
            high = data.astype(BF16).astype(F32)
            data = jnp.concatenate([high, data - high, high], 0).astype(BF16)
            product = dot(band, data)
            lines[d] = product[:, :lanes]
            lines[d + 1] = product[:, lanes:]

        def part(q, a):
            return lines[q, a * cols : (a + 1) * cols, :]

        def odd(u):
            return swap_halves(part(u, 0) + part(u + 1, 2) + part(u + 2, 4) + part(u + 3, 6))

        before = odd(0)
        for j in range(pairs):
            after = odd(j + 1)
            straight = part(j + 1, 1) + part(j + 2, 3) + part(j + 3, 5)
            field[j, t, 0:cols, :] = straight + jnp.where(low, before, after)
            before = after
        return carry

    lax.fori_loop(0, SPECIES, species, 0, unroll=4)

    def leave(j):
        rows = pl.ds(2 * j, 2)
        return pltpu.make_async_copy(ready.at[rows], out_ref.at[rows], done.at[j])

    def mixed(j, carry):
        smooth = [field[j, t, 0:cols, :] for t in range(SPECIES)]
        for p in range(SPECIES // 2):
            total = []
            for s in (2 * p, 2 * p + 1):
                acc = mix[s, 0] * smooth[0]
                for t in range(1, SPECIES):
                    acc = acc + mix[s, t] * smooth[t]
                total.append(acc)
            ready[2 * j, :, 128 * p : 128 * (p + 1)] = jnp.where(low, total[0], swap_halves(total[1]))
            ready[2 * j + 1, :, 128 * p : 128 * (p + 1)] = jnp.where(
                low, swap_halves(total[0]), total[1]
            )
        leave(j).start()
        return carry

    lax.fori_loop(0, pairs, mixed, 0, unroll=2)
    for j in range(pairs):
        leave(j).wait()


def shards(prior, obs_cell, obs_weight, obs_value, obs_var, loc_mask, batch_order, kernel, mixing):
    height, cols, channels = prior.shape
    across = lax.axis_size("cols")
    width = cols * across
    pairs = height // 2
    lanes = 2 * MEMBERS
    kept, sent = pl.pallas_call(
        functools.partial(gather_kernel, width),
        out_shape=(jax.ShapeDtypeStruct((2, OBS, lanes), F32),) * 2,
        in_specs=[SMEM, SMEM, VMEM, VMEM],
        out_specs=(VMEM, VMEM),
        scratch_shapes=[pltpu.VMEM((OBS, channels), F32)],
        compiler_params=PARAMS,
        name="gather",
    )(batch_order, obs_cell, jnp.transpose(obs_weight, (0, 2, 1)), prior)
    halo, parts = exchange(kept, sent, prior)
    return pl.pallas_call(
        functools.partial(forecast_kernel, width),
        out_shape=jax.ShapeDtypeStruct((height, cols, channels), F32),
        in_specs=[SMEM] * 5 + [VMEM] * 3 + [pl.BlockSpec(memory_space=pl.ANY)] + [VMEM] * 8,
        out_specs=pl.BlockSpec(memory_space=pl.ANY),
        scratch_shapes=[
            pltpu.VMEM((pairs + 3, SPECIES, cols + 8, lanes), F32),
            pltpu.VMEM((4, OBS, lanes), F32),
            pltpu.VMEM((24, OBS), F32),
            pltpu.VMEM((16, OBS), F32),
            pltpu.VMEM((3 * lanes, 2 * OBS), BF16),
            pltpu.VMEM((4 * OBS, 2 * lanes), BF16),
            pltpu.VMEM((3 * lanes, 2 * OBS), BF16),
            pltpu.VMEM((4 * OBS, 2 * lanes), BF16),
            pltpu.VMEM((pairs + 4, KW * cols, lanes), F32),
            pltpu.VMEM((height, cols, channels), F32),
            pltpu.VMEM((height, cols, channels), F32),
            pltpu.SemaphoreType.DMA,
            pltpu.SemaphoreType.DMA((pairs,)),
        ],
        compiler_params=PARAMS,
        name="forecast",
    )(
        batch_order, obs_cell, loc_mask, jnp.transpose(kernel, (1, 0, 2)), mixing,
        obs_cell, obs_value, obs_var, prior, *halo, *parts,
    )


def solution(mesh):
    return jax.shard_map(
        shards,
        mesh=mesh,
        in_specs=(P("rows", "cols", None), P(), P(), P(), P(), P(), P(), P(), P()),
        out_specs=P("rows", "cols", None),
        check_vma=False,
    )
```
